512 devices in a mesh: row: 16 (over y, z_hi, core), col: 32 (over z_lo, x).
Axes of the slice: x: 4, y: 4, z: 16 (z_hi: 2, z_lo: 8; z = z_hi * 8 + z_lo), core: 2. Of those that a mesh axis runs over, the one named last changes fastest.
Arguments:
- images: bfloat16 [4096, 1024], P(('row', 'col')), may hold values from -6 to 6
- texts: bfloat16 [4096, 1024], P(('row', 'col')), may hold values from -6 to 6
- loss_weights: float32 [2], replicated, may hold values from 0.5 to 1.5
Outputs:
- grad_images: float32 [4096, 1024], P(('row', 'col'))
- grad_texts: float32 [4096, 1024], P(('row', 'col'))
The draws below stay inside these ranges and needn't reach their ends.
All inputs are finite; a program needn't handle non-finite values.
Results may differ from the reference program's by a relative error of at most 0.0013.
Values may be sent and summed in bfloat16 or wider, within the bound.
A program may use at most 64 MiB of HBM per device.

```python
import math
import jax
import jax.numpy as jnp
from jax import lax

D = 1024
BATCH = 4096
ROW_BLOCK = 256


def levels(rng, extent, shards, least, high):
    loudness, own = 1.0, jax.random.fold_in(rng, 6)
    for dim, parts in shards:
        draws = jnp.exp(jax.random.uniform(jax.random.fold_in(own, dim), (parts,), jnp.float32, least / len(shards), high / len(shards)))
        loudness = loudness * jnp.repeat(draws, extent[dim] // parts).reshape([-1 if axis == dim else 1 for axis in range(len(extent))])
    return loudness


def bell_draw(stream_key, extent, scale, limit, pieces=(), kind=jnp.bfloat16):
    result = scale * jax.random.normal(stream_key, extent, jnp.float32)
    if pieces:
        result = result * levels(stream_key, extent, pieces, -0.22, 0.18)
    return jnp.clip(result, -limit, limit).astype(kind)


def setup_inputs(seed: int = 0) -> dict:
    streams_of = jax.random.split(jax.random.key(seed), 4)
    images = bell_draw(streams_of[0], (BATCH, D), 1.0, 6.0, ((0, 512),))
    texts = bell_draw(streams_of[1], (BATCH, D), 1.0, 6.0, ((0, 512),))
    loss_weights = jnp.clip(jax.random.uniform(streams_of[2], (2,), jnp.float32, 0.5, 1.5), 0.5, 1.5)
    return {"images": images, "texts": texts, "loss_weights": loss_weights}


def reference(images, texts, loss_weights):
    scale = 1.0 / math.sqrt(D * BATCH)
    cross_scale = loss_weights[0] * scale
    inner_scale = loss_weights[1] * scale
    stacked = jnp.concatenate([images, texts], axis=1).reshape(BATCH // ROW_BLOCK, ROW_BLOCK, 2 * D)

    def one_block(rows):
        rows_img = rows[:, :D]
        rows_txt = rows[:, D:]
        cross = jnp.dot(rows_img, texts.T, preferred_element_type=jnp.float32) - jnp.dot(rows_txt, images.T, preferred_element_type=jnp.float32)
        inmodal = jnp.dot(rows_img, images.T, preferred_element_type=jnp.float32) - jnp.dot(rows_txt, texts.T, preferred_element_type=jnp.float32)
        p_mat = (cross * cross_scale).astype(jnp.bfloat16)
        q_mat = (inmodal * inner_scale).astype(jnp.bfloat16)
        grad_img = jnp.dot(p_mat, texts, preferred_element_type=jnp.float32) + jnp.dot(q_mat, images, preferred_element_type=jnp.float32)
        grad_txt = -jnp.dot(p_mat, images, preferred_element_type=jnp.float32) - jnp.dot(q_mat, texts, preferred_element_type=jnp.float32)
        return (grad_img, grad_txt)
    grad_img, grad_txt = lax.map(one_block, stacked)
    return (grad_img.reshape(BATCH, D), grad_txt.reshape(BATCH, D))
```

```python
import functools
import math

import jax
import jax.numpy as jnp
from jax import lax
from jax.experimental import pallas as pl
from jax.experimental.pallas import tpu as pltpu
from jax.sharding import PartitionSpec as P

MESH = pl.DeviceIdType.MESH
NX, NY, NZ, CORES = 4, 4, 16, 2
HALF = NZ // 2


def ring_distance(step, size):
    return min(step, size - step)


PLANE = sorted(
    [(dx, dy) for dy in range(NY) for dx in range(NX)],
    key=lambda o: -(ring_distance(o[0], NX) + ring_distance(o[1], NY)),
)
PEERS = len(PLANE) - 1


def kernel(scale, weights, img, txt, out, xi, xj, w, part, inbox, up_send, up_recv, down_send, down_recv, sib_send, sib_recv, i_send, i_recv, g_send, g_recv):
    rows, width = xi.shape[1:]
    half = width // 2
    row, col = lax.axis_index("row"), lax.axis_index("col")
    y, zh, core = row // 4, (row // 2) % 2, row % 2
    zl, x = col // NX, col % NX
    z = zh * 8 + zl

    def device(x, y, z, core):
        return (y * 4 + (z // 8) * 2 + core, (z % 8) * NX + x)

    above = device(x, y, (z + 1) % NZ, core)
    below = device(x, y, (z + NZ - 1) % NZ, core)
    sibling = device(x, y, z, 1 - core)
    ahead = [device((x + dx) % NX, (y + dy) % NY, z, core) for dx, dy in PLANE[:PEERS]]
    behind = [device((x + NX - dx) % NX, (y + NY - dy) % NY, z, core) for dx, dy in PLANE[:PEERS]]

    own = jnp.concatenate([img[...].astype(jnp.float32), txt[...].astype(jnp.float32)], axis=0).astype(jnp.bfloat16)
    xj[0] = own
    xi[PEERS] = own

    barrier = pltpu.get_barrier_semaphore()
    for peer in [above, below, sibling] + ahead:
        pl.semaphore_signal(barrier, inc=1, device_id=peer, device_id_type=MESH)
    pl.semaphore_wait(barrier, 3 + PEERS)

    def piece(slot, h):
        return xj.at[slot, :, pl.ds(h * half, half)]

    def hop(up, d, h):
        src, dst = (d - 1, d) if up else ((NZ - d + 1) % NZ, NZ - d)
        send, recv = (up_send, up_recv) if up else (down_send, down_recv)
        return pltpu.make_async_remote_copy(
            src_ref=piece(src, h), dst_ref=piece(dst, h), send_sem=send.at[d - 1, h], recv_sem=recv.at[d - 1, h],
            device_id=above if up else below, device_id_type=MESH)

    def across(slot, h):
        return pltpu.make_async_remote_copy(
            src_ref=piece(slot, h), dst_ref=piece(slot + NZ, h), send_sem=sib_send.at[slot, h], recv_sem=sib_recv.at[slot, h],
            device_id=sibling, device_id_type=MESH)

    def spread(k):
        return pltpu.make_async_remote_copy(
            src_ref=xi.at[PEERS], dst_ref=xi.at[k], send_sem=i_send.at[k], recv_sem=i_recv.at[k],
            device_id=ahead[k], device_id_type=MESH)

    def give(k):
        return pltpu.make_async_remote_copy(
            src_ref=part.at[k], dst_ref=inbox.at[k], send_sem=g_send.at[k], recv_sem=g_recv.at[k],
            device_id=behind[k], device_id_type=MESH)

    def moves(d):
        listed = [(True, 0), (False, 1)]
        if d < HALF:
            listed += [(True, 1), (False, 0)]
        return listed

    for up, h in moves(1):
        hop(up, 1, h).start()
    for h in range(2):
        across(0, h).start()
    for k in range(PEERS):
        spread(k).start()
    for d in range(1, HALF + 1):
        for up, h in moves(d):
            hop(up, d, h).wait_recv()
            if d < HALF and (up, h) in moves(d + 1):
                hop(up, d + 1, h).start()
            across(d if up else NZ - d, h).start()
    for k in range(PEERS):
        spread(k).wait_recv()
    for slot in range(NZ):
        for h in range(2):
            across(slot, h).wait_recv()

    blocks = PEERS + 1
    keys = xj[...].reshape(2 * NZ * rows, width)
    scores = lax.dot_general(
        xi[...].reshape(blocks * rows, width), keys, (((1,), (1,)), ((), ())), preferred_element_type=jnp.float32)
    lanes = scores.shape[1]
    lane_kind = (lax.broadcasted_iota(jnp.int32, scores.shape, 1) // 8) % 2
    row_kind = (lax.broadcasted_iota(jnp.int32, scores.shape, 0) // 8) % 2
    turned = jnp.where(lane_kind == 0, pltpu.roll(scores, lanes - 8, 1), pltpu.roll(scores, 8, 1))
    turned = turned.reshape(blocks, 2, 8, lanes)
    turned = jnp.concatenate([turned[:, 1:], turned[:, :1]], axis=1).reshape(scores.shape)
    factor = jnp.where(lane_kind == row_kind, weights[1] * scale, weights[0] * scale)
    w[...] = ((scores - turned) * factor).astype(jnp.bfloat16)

    group = 4
    for first in range(0, blocks, group):
        total = jnp.dot(w[pl.ds(first * rows, group * rows), :], keys, preferred_element_type=jnp.float32)
        for k in range(first, first + group):
            block = total[(k - first) * rows : (k - first + 1) * rows]
            if k < PEERS:
                part[k] = block.astype(jnp.bfloat16)
                give(k).start()
            else:
                mine = block
    for k in range(PEERS):
        give(k).wait_recv()
        mine = mine + inbox[k].astype(jnp.float32)
    out[0] = mine[:8]
    out[1] = mine[8:]

    for d in range(1, HALF + 1):
        for up, h in moves(d):
            hop(up, d, h).wait_send()
    for slot in range(NZ):
        for h in range(2):
            across(slot, h).wait_send()
    for k in range(PEERS):
        spread(k).wait_send()
        give(k).wait_send()


def local(images, texts, loss_weights):
    count, width = images.shape
    batch = count * lax.axis_size("row") * lax.axis_size("col")
    scale = 1.0 / math.sqrt(width * batch)
    rows = 2 * count
    dma = pltpu.SemaphoreType.DMA
    grads = pl.pallas_call(
        functools.partial(kernel, scale),
        out_shape=jax.ShapeDtypeStruct((2, count, width), jnp.float32),
        in_specs=[pl.BlockSpec(memory_space=pltpu.SMEM)] + [pl.BlockSpec(memory_space=pltpu.VMEM)] * 2,
        out_specs=pl.BlockSpec(memory_space=pltpu.VMEM),
        scratch_shapes=[
            pltpu.VMEM((PEERS + 1, rows, width), jnp.bfloat16),
            pltpu.VMEM((2 * NZ, rows, width), jnp.bfloat16),
            pltpu.VMEM(((PEERS + 1) * rows, 2 * NZ * rows), jnp.bfloat16),
            pltpu.VMEM((PEERS, rows, width), jnp.bfloat16),
            pltpu.VMEM((PEERS, rows, width), jnp.bfloat16),
            dma((HALF, 2)), dma((HALF, 2)), dma((HALF, 2)), dma((HALF, 2)),
            dma((NZ, 2)), dma((NZ, 2)),
            dma((PEERS,)), dma((PEERS,)), dma((PEERS,)), dma((PEERS,)),
        ],
        compiler_params=pltpu.CompilerParams(collective_id=0, has_side_effects=True, vmem_limit_bytes=32 * 1024 * 1024),
    )(loss_weights, images, texts)
    return (grads[0], grads[1])


def solution(mesh):
    in_specs = (P(("row", "col"), None), P(("row", "col"), None), P())
    out_specs = (P(("row", "col"), None), P(("row", "col"), None))
    return jax.shard_map(local, mesh=mesh, in_specs=in_specs, out_specs=out_specs, check_vma=False)
```

```python
import functools
import math

import jax
import jax.numpy as jnp
from jax import lax
from jax.experimental import pallas as pl
from jax.experimental.pallas import tpu as pltpu
from jax.sharding import PartitionSpec as P

MESH = pl.DeviceIdType.MESH
NX, NY, NZ, CORES = 4, 4, 16, 2
HALF = NZ // 2


def ring_distance(step, size):
    return min(step, size - step)


PLANE = sorted(
    [(dx, dy) for dy in range(NY) for dx in range(NX)],
    key=lambda o: -(ring_distance(o[0], NX) + ring_distance(o[1], NY)),
)
PEERS = len(PLANE) - 1

NEAR = [(0, 5), (0, 2), (0, 1), (2, 1), (5, 3), (5, 2), (5, 1), (5, -1)]
HOPS = [hop for origin, step in NEAR for hop in ((origin, step), (-origin, -step))]
LINE_PEERS = sorted({step for _, step in HOPS})
ARRIVALS = [hop for origin, step in [(0, 2), (0, 5), (0, 1), (2, 1), (5, 1), (5, -1), (5, 2), (5, 3)] for hop in ((origin, step), (-origin, -step))]


def kernel(scale, weights_hbm, img_hbm, txt_hbm, out, weights, img, txt, xi, xj, w, part, inbox, load_sem, z_send, z_recv, sib_send, sib_recv, i_send, i_recv, g_send, g_recv):
    rows, width = xi.shape[1:]
    half = width // 2
    row, col = lax.axis_index("row"), lax.axis_index("col")
    y, zh, core = row // 4, (row // 2) % 2, row % 2
    zl, x = col // NX, col % NX
    z = zh * 8 + zl

    def device(x, y, z, core):
        return (y * 4 + (z // 8) * 2 + core, (z % 8) * NX + x)

    sibling = device(x, y, z, 1 - core)
    line = {d: device(x, y, (z + d + NZ) % NZ, core) for d in LINE_PEERS}
    ahead = [device((x + dx) % NX, (y + dy) % NY, z, core) for dx, dy in PLANE[:PEERS]]
    behind = [device((x + NX - dx) % NX, (y + NY - dy) % NY, z, core) for dx, dy in PLANE[:PEERS]]

    barrier = pltpu.get_barrier_semaphore()
    for peer in list(line.values()) + [sibling] + ahead:
        pl.semaphore_signal(barrier, inc=1, device_id=peer, device_id_type=MESH)

    loads = [
        pltpu.make_async_copy(img_hbm, img, load_sem.at[0]),
        pltpu.make_async_copy(txt_hbm, txt, load_sem.at[1]),
        pltpu.make_async_copy(weights_hbm, weights, load_sem.at[2]),
    ]
    for load in loads:
        load.start()
    for load in loads:
        load.wait()
    own = jnp.concatenate([img[...].astype(jnp.float32), txt[...].astype(jnp.float32)], axis=0).astype(jnp.bfloat16)
    xj[0] = own
    xi[PEERS] = own
    pl.semaphore_wait(barrier, len(line) + 1 + PEERS)

    def hop(origin, step):
        src, dst = origin % NZ, (origin + step) % NZ
        k = HOPS.index((origin, step))
        part = slice(None) if dst != HALF else pl.ds(0 if step > 0 else half, half)
        return pltpu.make_async_remote_copy(
            src_ref=xj.at[src, :, part], dst_ref=xj.at[dst, :, part], send_sem=z_send.at[k], recv_sem=z_recv.at[k],
            device_id=line[step], device_id_type=MESH)

    def across(slot):
        return pltpu.make_async_remote_copy(
            src_ref=xj.at[slot], dst_ref=xj.at[slot + NZ], send_sem=sib_send.at[slot], recv_sem=sib_recv.at[slot],
            device_id=sibling, device_id_type=MESH)

    def spread(k):
        return pltpu.make_async_remote_copy(
            src_ref=xi.at[PEERS], dst_ref=xi.at[k], send_sem=i_send.at[k], recv_sem=i_recv.at[k],
            device_id=ahead[k], device_id_type=MESH)

    def give(k):
        return pltpu.make_async_remote_copy(
            src_ref=part.at[k], dst_ref=inbox.at[k], send_sem=g_send.at[k], recv_sem=g_recv.at[k],
            device_id=behind[k], device_id_type=MESH)

    for origin, step in HOPS:
        if origin == 0:
            hop(0, step).start()
    across(0).start()
    for k in range(PEERS):
        spread(k).start()
    for origin, step in ARRIVALS:
        hop(origin, step).wait_recv()
        here = origin + step
        for onward in HOPS:
            if onward[0] == here:
                hop(*onward).start()
        if abs(here) != HALF:
            across(here % NZ).start()
    across(HALF).start()
    for k in range(PEERS):
        spread(k).wait_recv()
    for slot in range(NZ):
        across(slot).wait_recv()

    blocks = PEERS + 1
    keys = xj[...].reshape(2 * NZ * rows, width)
    scores = lax.dot_general(
        xi[...].reshape(blocks * rows, width), keys, (((1,), (1,)), ((), ())), preferred_element_type=jnp.float32)
    lanes = scores.shape[1]
    lane_kind = (lax.broadcasted_iota(jnp.int32, scores.shape, 1) // 8) % 2
    row_kind = (lax.broadcasted_iota(jnp.int32, scores.shape, 0) // 8) % 2
    turned = jnp.where(lane_kind == 0, pltpu.roll(scores, lanes - 8, 1), pltpu.roll(scores, 8, 1))
    turned = turned.reshape(blocks, 2, 8, lanes)
    turned = jnp.concatenate([turned[:, 1:], turned[:, :1]], axis=1).reshape(scores.shape)
    factor = jnp.where(lane_kind == row_kind, weights[1] * scale, weights[0] * scale)
    w[...] = ((scores - turned) * factor).astype(jnp.bfloat16)

    group = 4
    for first in range(0, blocks, group):
        total = jnp.dot(w[pl.ds(first * rows, group * rows), :], keys, preferred_element_type=jnp.float32)
        for k in range(first, first + group):
            block = total[(k - first) * rows : (k - first + 1) * rows]
            if k < PEERS:
                part[k] = block.astype(jnp.bfloat16)
                give(k).start()
            else:
                mine = block
    for k in range(PEERS):
        give(k).wait_recv()
        mine = mine + inbox[k].astype(jnp.float32)
    out[0] = mine[:8]
    out[1] = mine[8:]

    for origin, step in HOPS:
        hop(origin, step).wait_send()
    for slot in range(NZ):
        across(slot).wait_send()
    for k in range(PEERS):
        spread(k).wait_send()
        give(k).wait_send()


def local(images, texts, loss_weights):
    count, width = images.shape
    batch = count * lax.axis_size("row") * lax.axis_size("col")
    scale = 1.0 / math.sqrt(width * batch)
    rows = 2 * count
    dma = pltpu.SemaphoreType.DMA
    grads = pl.pallas_call(
        functools.partial(kernel, scale),
        out_shape=jax.ShapeDtypeStruct((2, count, width), jnp.float32),
        in_specs=[pl.BlockSpec(memory_space=pl.ANY)] * 3,
        out_specs=pl.BlockSpec(memory_space=pltpu.VMEM),
        scratch_shapes=[
            pltpu.SMEM((2,), jnp.float32),
            pltpu.VMEM((count, width), jnp.bfloat16),
            pltpu.VMEM((count, width), jnp.bfloat16),
            pltpu.VMEM((PEERS + 1, rows, width), jnp.bfloat16),
            pltpu.VMEM((2 * NZ, rows, width), jnp.bfloat16),
            pltpu.VMEM(((PEERS + 1) * rows, 2 * NZ * rows), jnp.bfloat16),
            pltpu.VMEM((PEERS, rows, width), jnp.bfloat16),
            pltpu.VMEM((PEERS, rows, width), jnp.bfloat16),
            dma((3,)),
            dma((len(HOPS),)), dma((len(HOPS),)),
            dma((NZ,)), dma((NZ,)),
            dma((PEERS,)), dma((PEERS,)), dma((PEERS,)), dma((PEERS,)),
        ],
        compiler_params=pltpu.CompilerParams(collective_id=0, has_side_effects=True),
    )(loss_weights, images, texts)
    return (grads[0], grads[1])


def solution(mesh):
    in_specs = (P(("row", "col"), None), P(("row", "col"), None), P())
    out_specs = (P(("row", "col"), None), P(("row", "col"), None))
    return jax.shard_map(local, mesh=mesh, in_specs=in_specs, out_specs=out_specs, check_vma=False)
```

```python
import functools
import math

import jax
import jax.numpy as jnp
from jax import lax
from jax.experimental import pallas as pl
from jax.experimental.pallas import tpu as pltpu
from jax.sharding import PartitionSpec as P

MESH = pl.DeviceIdType.MESH
NX, NY, NZ, CORES = 4, 4, 16, 2
HALF = NZ // 2


def ring_distance(step, size):
    return min(step, size - step)


PLANE = sorted(
    [(dx, dy) for dy in range(NY) for dx in range(NX)],
    key=lambda o: -(ring_distance(o[0], NX) + ring_distance(o[1], NY)),
)
PEERS = len(PLANE) - 1

NEAR = [(0, 5), (0, 2), (0, 1), (2, 1), (5, 3), (5, 2), (5, 1), (5, -1)]
HOPS = [hop for origin, step in NEAR for hop in ((origin, step), (-origin, -step))]
LINE_PEERS = sorted({step for _, step in HOPS})
ARRIVALS = [[(0, 2)], [(0, -2)], [(0, 5)], [(0, -5)]] + [
    [(origin, step), (-origin, -step)] for origin, step in [(0, 1), (2, 1), (5, 1), (5, -1), (5, 2), (5, 3)]
]
GROUPS = [group[0] for group in ARRIVALS]


def kernel(scale, weights_hbm, img_hbm, txt_hbm, out, weights, own, xi, xj, w, part, inbox, load_sem, z_send, z_recv, sib_send, sib_recv, i_send, i_recv, g_send, g_recv):
    rows, width = xi.shape[1:]
    half = width // 2
    row, col = lax.axis_index("row"), lax.axis_index("col")
    y, zh, core = row // 4, (row // 2) % 2, row % 2
    zl, x = col // NX, col % NX
    z = zh * 8 + zl

    def device(x, y, z, core):
        return (y * 4 + (z // 8) * 2 + core, (z % 8) * NX + x)

    sibling = device(x, y, z, 1 - core)
    line = {d: device(x, y, (z + d + NZ) % NZ, core) for d in LINE_PEERS}
    ahead = [device((x + dx) % NX, (y + dy) % NY, z, core) for dx, dy in PLANE[:PEERS]]
    behind = [device((x + NX - dx) % NX, (y + NY - dy) % NY, z, core) for dx, dy in PLANE[:PEERS]]

    barrier = pltpu.get_barrier_semaphore()
    for peer in list(line.values()) + [sibling] + ahead:
        pl.semaphore_signal(barrier, inc=1, device_id=peer, device_id_type=MESH)

    loads = [
        pltpu.make_async_copy(img_hbm, own.at[0], load_sem.at[0]),
        pltpu.make_async_copy(txt_hbm, own.at[1], load_sem.at[1]),
        pltpu.make_async_copy(weights_hbm, weights, load_sem.at[2]),
    ]
    for load in loads:
        load.start()
    for load in loads:
        load.wait()
    block = own[...].astype(jnp.float32).reshape(rows, width).astype(jnp.bfloat16)
    xj[0] = block
    xi[PEERS] = block
    pl.semaphore_wait(barrier, len(line) + 1 + PEERS)

    def hop(origin, step):
        src, dst = origin % NZ, (origin + step) % NZ
        k = GROUPS.index((origin, step)) if (origin, step) in GROUPS else GROUPS.index((-origin, -step))
        part = slice(None) if dst != HALF else pl.ds(0 if step > 0 else half, half)
        return pltpu.make_async_remote_copy(
            src_ref=xj.at[src, :, part], dst_ref=xj.at[dst, :, part], send_sem=z_send, recv_sem=z_recv.at[k],
            device_id=line[step], device_id_type=MESH)

    def across(slot):
        return pltpu.make_async_remote_copy(
            src_ref=xj.at[slot], dst_ref=xj.at[slot + NZ], send_sem=sib_send, recv_sem=sib_recv,
            device_id=sibling, device_id_type=MESH)

    def spread(k):
        return pltpu.make_async_remote_copy(
            src_ref=xi.at[PEERS], dst_ref=xi.at[k], send_sem=i_send, recv_sem=i_recv,
            device_id=ahead[k], device_id_type=MESH)

    def give(k):
        return pltpu.make_async_remote_copy(
            src_ref=part.at[k], dst_ref=inbox.at[k], send_sem=g_send, recv_sem=g_recv,
            device_id=behind[k], device_id_type=MESH)

    def landed(ref, sem):
        pltpu.make_async_copy(ref, ref, sem).wait()

    for origin, step in HOPS:
        if origin == 0:
            hop(0, step).start()
    across(0).start()
    for k in range(PEERS):
        spread(k).start()
    for group in ARRIVALS:
        landed(xj.at[pl.ds(0, len(group))] if group[0] != (5, 3) else xj.at[0], z_recv.at[GROUPS.index(group[0])])
        for origin, step in group:
            here = origin + step
            for onward in HOPS:
                if onward[0] == here:
                    hop(*onward).start()
            if abs(here) != HALF:
                across(here % NZ).start()
    across(HALF).start()
    landed(xi.at[pl.ds(0, PEERS)], i_recv)
    landed(xj.at[pl.ds(NZ, NZ)], sib_recv)

    blocks = PEERS + 1
    keys = xj[...].reshape(2 * NZ * rows, width)
    scores = lax.dot_general(
        xi[...].reshape(blocks * rows, width), keys, (((1,), (1,)), ((), ())), preferred_element_type=jnp.float32)
    lanes = scores.shape[1]
    lane_kind = (lax.broadcasted_iota(jnp.int32, scores.shape, 1) // 8) % 2
    row_kind = (lax.broadcasted_iota(jnp.int32, scores.shape, 0) // 8) % 2
    turned = jnp.where(lane_kind == 0, pltpu.roll(scores, lanes - 8, 1), pltpu.roll(scores, 8, 1))
    turned = turned.reshape(blocks, 2, 8, lanes)
    turned = jnp.concatenate([turned[:, 1:], turned[:, :1]], axis=1).reshape(scores.shape)
    factor = jnp.where(lane_kind == row_kind, weights[1] * scale, weights[0] * scale)
    w[...] = ((scores - turned) * factor).astype(jnp.bfloat16)

    group = 4
    for first in range(0, blocks, group):
        total = jnp.dot(w[pl.ds(first * rows, group * rows), :], keys, preferred_element_type=jnp.float32)
        for k in range(first, first + group):
            block = total[(k - first) * rows : (k - first + 1) * rows]
            if k < PEERS:
                part[k] = block.astype(jnp.bfloat16)
                give(k).start()
            else:
                mine = block
    landed(inbox, g_recv)
    for k in range(PEERS):
        mine = mine + inbox[k].astype(jnp.float32)
    out[0] = mine[:8]
    out[1] = mine[8:]

    landed(xj.at[pl.ds(0, NZ - 1)], z_send)
    landed(xj.at[pl.ds(0, NZ)], sib_send)
    landed(xi.at[pl.ds(0, PEERS)], i_send)
    landed(part, g_send)


def local(images, texts, loss_weights):
    count, width = images.shape
    batch = count * lax.axis_size("row") * lax.axis_size("col")
    scale = 1.0 / math.sqrt(width * batch)
    rows = 2 * count
    dma = pltpu.SemaphoreType.DMA
    grads = pl.pallas_call(
        functools.partial(kernel, scale),
        out_shape=pltpu.VMEM((2, count, width), jnp.float32),
        in_specs=[pl.BlockSpec(memory_space=pltpu.HBM)] * 3,
        out_specs=pl.BlockSpec(memory_space=pltpu.VMEM),
        scratch_shapes=[
            pltpu.SMEM((2,), jnp.float32),
            pltpu.VMEM((2, count, width), jnp.bfloat16),
            pltpu.VMEM((PEERS + 1, rows, width), jnp.bfloat16),
            pltpu.VMEM((2 * NZ, rows, width), jnp.bfloat16),
            pltpu.VMEM(((PEERS + 1) * rows, 2 * NZ * rows), jnp.bfloat16),
            pltpu.VMEM((PEERS, rows, width), jnp.bfloat16),
            pltpu.VMEM((PEERS, rows, width), jnp.bfloat16),
            dma((3,)),
            dma, dma((len(GROUPS),)),
            dma, dma, dma, dma, dma, dma,
        ],
        compiler_params=pltpu.CompilerParams(collective_id=0, has_side_effects=True, vmem_limit_bytes=60 * 1024 * 1024),
    )(loss_weights, images, texts)
    return (grads[0], grads[1])


def solution(mesh):
    in_specs = (P(("row", "col"), None), P(("row", "col"), None), P())
    out_specs = (P(("row", "col"), None), P(("row", "col"), None))
    return jax.shard_map(local, mesh=mesh, in_specs=in_specs, out_specs=out_specs, check_vma=False)
```

```python
import functools
import math

import jax
import jax.numpy as jnp
from jax import lax
from jax.experimental import pallas as pl
from jax.experimental.pallas import tpu as pltpu
from jax.sharding import PartitionSpec as P

MESH = pl.DeviceIdType.MESH
NX, NY, NZ, CORES = 4, 4, 16, 2
HALF = NZ // 2
EARLY = NZ // 2


def ring_distance(step, size):
    return min(step, size - step)


PLANE = sorted(
    [(dx, dy) for dy in range(NY) for dx in range(NX)],
    key=lambda o: -(ring_distance(o[0], NX) + ring_distance(o[1], NY)),
)
PEERS = len(PLANE) - 1

NEAR = [(0, 5), (0, 2), (0, 1), (2, 1), (5, 3), (5, 2), (5, 1), (5, -1)]
HOPS = [hop for origin, step in NEAR for hop in ((origin, step), (-origin, -step))]
LINE_PEERS = sorted({step for _, step in HOPS})
ARRIVALS = [[(0, 2)], [(0, -2)], [(0, 5)], [(0, -5)]] + [
    [(origin, step), (-origin, -step)] for origin, step in [(0, 1), (2, 1), (5, 1), (5, -1), (5, 2), (5, 3)]
]
GROUPS = [group[0] for group in ARRIVALS]


def kernel(scale, weights_hbm, img_hbm, txt_hbm, out, weights, own, xi, xj, w, part, inbox, entered, load_sem, z_send, z_recv, sib_send, sib_recv, i_send, i_recv, g_send, g_recv):
    rows, width = xi.shape[1:]
    half = width // 2
    row, col = lax.axis_index("row"), lax.axis_index("col")
    y, zh, core = row // 4, (row // 2) % 2, row % 2
    zl, x = col // NX, col % NX
    z = zh * 8 + zl

    def device(x, y, z, core):
        return (y * 4 + (z // 8) * 2 + core, (z % 8) * NX + x)

    sibling = device(x, y, z, 1 - core)
    line = {d: device(x, y, (z + d + NZ) % NZ, core) for d in LINE_PEERS}
    ahead = [device((x + dx) % NX, (y + dy) % NY, z, core) for dx, dy in PLANE[:PEERS]]
    behind = [device((x + NX - dx) % NX, (y + NY - dy) % NY, z, core) for dx, dy in PLANE[:PEERS]]

    barrier = pltpu.get_barrier_semaphore()
    late = z // EARLY
    far_late = {d: ((z + d + NZ) % NZ) // EARLY for d in LINE_PEERS}
    late_peers = sum(far_late.values())
    for peer in [sibling] + ahead:
        pl.semaphore_signal(barrier, inc=1, device_id=peer, device_id_type=MESH)
    for d in LINE_PEERS:
        @pl.when(late * (1 - far_late[d]) == 0)
        def _():
            pl.semaphore_signal(barrier, inc=1, device_id=line[d], device_id_type=MESH)

    loads = [
        pltpu.make_async_copy(img_hbm, own.at[0], load_sem.at[0]),
        pltpu.make_async_copy(txt_hbm, own.at[1], load_sem.at[1]),
        pltpu.make_async_copy(weights_hbm, weights, load_sem.at[2]),
    ]
    for load in loads:
        load.start()
    for load in loads:
        load.wait()
    block = own[...].astype(jnp.float32).reshape(rows, width).astype(jnp.bfloat16)
    xj[0] = block
    xi[PEERS] = block
    pl.semaphore_wait(barrier, len(line) + 1 + PEERS - (1 - late) * late_peers)
    for d in LINE_PEERS:
        @pl.when(late * (1 - far_late[d]) == 1)
        def _():
            pl.semaphore_signal(entered, inc=1, device_id=line[d], device_id_type=MESH)

    def hop(origin, step):
        src, dst = origin % NZ, (origin + step) % NZ
        k = GROUPS.index((origin, step)) if (origin, step) in GROUPS else GROUPS.index((-origin, -step))
        part = slice(None) if dst != HALF else pl.ds(0 if step > 0 else half, half)
        return pltpu.make_async_remote_copy(
            src_ref=xj.at[src, :, part], dst_ref=xj.at[dst, :, part], send_sem=z_send, recv_sem=z_recv.at[k],
            device_id=line[step], device_id_type=MESH)

    def across(slot):
        return pltpu.make_async_remote_copy(
            src_ref=xj.at[slot], dst_ref=xj.at[slot + NZ], send_sem=sib_send, recv_sem=sib_recv,
            device_id=sibling, device_id_type=MESH)

    def spread(k):
        return pltpu.make_async_remote_copy(
            src_ref=xi.at[PEERS], dst_ref=xi.at[k], send_sem=i_send, recv_sem=i_recv,
            device_id=ahead[k], device_id_type=MESH)

    def give(k):
        return pltpu.make_async_remote_copy(
            src_ref=part.at[k], dst_ref=inbox.at[k], send_sem=g_send, recv_sem=g_recv,
            device_id=behind[k], device_id_type=MESH)

    def landed(ref, sem):
        pltpu.make_async_copy(ref, ref, sem).wait()

    def begin(waiting):
        for origin, step in HOPS:
            if origin == 0:
                pl.when((1 - late) * far_late[step] == waiting)(lambda step=step: hop(0, step).start())

    begin(0)
    across(0).start()
    for k in range(PEERS):
        spread(k).start()
    pl.when(late == 0)(lambda: pl.semaphore_wait(entered, late_peers))
    begin(1)
    for group in ARRIVALS:
        landed(xj.at[pl.ds(0, len(group))] if group[0] != (5, 3) else xj.at[0], z_recv.at[GROUPS.index(group[0])])
        for origin, step in group:
            here = origin + step
            for onward in HOPS:
                if onward[0] == here:
                    hop(*onward).start()
            if abs(here) != HALF:
                across(here % NZ).start()
    across(HALF).start()
    landed(xi.at[pl.ds(0, PEERS)], i_recv)
    landed(xj.at[pl.ds(NZ, NZ)], sib_recv)

    blocks = PEERS + 1
    keys = xj[...].reshape(2 * NZ * rows, width)
    scores = lax.dot_general(
        xi[...].reshape(blocks * rows, width), keys, (((1,), (1,)), ((), ())), preferred_element_type=jnp.float32)
    lanes = scores.shape[1]
    lane_kind = (lax.broadcasted_iota(jnp.int32, scores.shape, 1) // 8) % 2
    row_kind = (lax.broadcasted_iota(jnp.int32, scores.shape, 0) // 8) % 2
    turned = jnp.where(lane_kind == 0, pltpu.roll(scores, lanes - 8, 1), pltpu.roll(scores, 8, 1))
    turned = turned.reshape(blocks, 2, 8, lanes)
    turned = jnp.concatenate([turned[:, 1:], turned[:, :1]], axis=1).reshape(scores.shape)
    factor = jnp.where(lane_kind == row_kind, weights[1] * scale, weights[0] * scale)
    w[...] = ((scores - turned) * factor).astype(jnp.bfloat16)

    group = 4
    for first in range(0, blocks, group):
        total = jnp.dot(w[pl.ds(first * rows, group * rows), :], keys, preferred_element_type=jnp.float32)
        for k in range(first, first + group):
            block = total[(k - first) * rows : (k - first + 1) * rows]
            if k < PEERS:
                part[k] = block.astype(jnp.bfloat16)
                give(k).start()
            else:
                mine = block
    landed(inbox, g_recv)
    for k in range(PEERS):
        mine = mine + inbox[k].astype(jnp.float32)
    out[0] = mine[:8]
    out[1] = mine[8:]

    landed(xj.at[pl.ds(0, NZ - 1)], z_send)
    landed(xj.at[pl.ds(0, NZ)], sib_send)
    landed(xi.at[pl.ds(0, PEERS)], i_send)
    landed(part, g_send)


def local(images, texts, loss_weights):
    count, width = images.shape
    batch = count * lax.axis_size("row") * lax.axis_size("col")
    scale = 1.0 / math.sqrt(width * batch)
    rows = 2 * count
    dma = pltpu.SemaphoreType.DMA
    grads = pl.pallas_call(
        functools.partial(kernel, scale),
        out_shape=pltpu.VMEM((2, count, width), jnp.float32),
        in_specs=[pl.BlockSpec(memory_space=pltpu.HBM)] * 3,
        out_specs=pl.BlockSpec(memory_space=pltpu.VMEM),
        scratch_shapes=[
            pltpu.SMEM((2,), jnp.float32),
            pltpu.VMEM((2, count, width), jnp.bfloat16),
            pltpu.VMEM((PEERS + 1, rows, width), jnp.bfloat16),
            pltpu.VMEM((2 * NZ, rows, width), jnp.bfloat16),
            pltpu.VMEM(((PEERS + 1) * rows, 2 * NZ * rows), jnp.bfloat16),
            pltpu.VMEM((PEERS, rows, width), jnp.bfloat16),
            pltpu.VMEM((PEERS, rows, width), jnp.bfloat16),
            pltpu.SemaphoreType.REGULAR,
            dma((3,)),
            dma, dma((len(GROUPS),)),
            dma, dma, dma, dma, dma, dma,
        ],
        compiler_params=pltpu.CompilerParams(collective_id=0, has_side_effects=True, vmem_limit_bytes=60 * 1024 * 1024),
    )(loss_weights, images, texts)
    return (grads[0], grads[1])


def solution(mesh):
    in_specs = (P(("row", "col"), None), P(("row", "col"), None), P())
    out_specs = (P(("row", "col"), None), P(("row", "col"), None))
    return jax.shard_map(local, mesh=mesh, in_specs=in_specs, out_specs=out_specs, check_vma=False)
```

```python
import functools
import math

import jax
import jax.numpy as jnp
from jax import lax
from jax.experimental import pallas as pl
from jax.experimental.pallas import tpu as pltpu
from jax.sharding import PartitionSpec as P

MESH = pl.DeviceIdType.MESH
NX, NY, NZ, CORES = 4, 4, 16, 2
HALF = NZ // 2


def ring_distance(step, size):
    return min(step, size - step)


PLANE = sorted(
    [(dx, dy) for dy in range(NY) for dx in range(NX)],
    key=lambda o: -(ring_distance(o[0], NX) + ring_distance(o[1], NY)),
)
PEERS = len(PLANE) - 1

NEAR = [(0, 5), (0, 2), (0, 1), (2, 1), (5, 3), (5, 2), (5, 1), (5, -1)]
HOPS = [hop for origin, step in NEAR for hop in ((origin, step), (-origin, -step))]
LINE_PEERS = sorted({step for _, step in HOPS})


def arrivals():
    level, order = {0: 0}, []
    for origin, step in NEAR:
        level[origin + step] = level[origin] + 1
    relays = [hop for hop in NEAR if any(origin == sum(hop) for origin, _ in NEAR)]
    for depth in sorted({level[sum(hop)] for hop in relays}):
        for c in (1, 0):
            for origin, step in relays:
                if level[origin + step] == depth:
                    order += [[(origin, step, c)], [(-origin, -step, c)]]
    for origin, step in sorted(set(NEAR) - set(relays), key=lambda hop: level[sum(hop)]):
        order.append([(origin, step, 1), (origin, step, 0), (-origin, -step, 1), (-origin, -step, 0)])
    return order


ARRIVALS = arrivals()


def group_of(origin, step, c):
    return next(n for n, group in enumerate(ARRIVALS) if (origin, step, c) in group)


def kernel(scale, weights_hbm, img_hbm, txt_hbm, out, weights, own, xi, xj, w, part, inbox, load_sem, z_send, z_recv, hand_send, hand_recv, sib_send, sib_recv, i_send, i_recv, g_send, g_recv):
    rows, width = xi.shape[1:]
    half = width // 2
    row, col = lax.axis_index("row"), lax.axis_index("col")
    y, zh, core = row // 4, (row // 2) % 2, row % 2
    zl, x = col // NX, col % NX
    z = zh * 8 + zl

    def device(x, y, z, core):
        return (y * 4 + (z // 8) * 2 + core, (z % 8) * NX + x)

    sibling = device(x, y, z, 1 - core)
    line = {d: device(x, y, (z + d + NZ) % NZ, core) for d in LINE_PEERS}
    ahead = [device((x + dx) % NX, (y + dy) % NY, z, core) for dx, dy in PLANE[:PEERS]]
    behind = [device((x + NX - dx) % NX, (y + NY - dy) % NY, z, core) for dx, dy in PLANE[:PEERS]]

    barrier = pltpu.get_barrier_semaphore()
    for peer in [sibling] + ahead:
        pl.semaphore_signal(barrier, inc=1, device_id=peer, device_id_type=MESH)

    @pl.when(core == 1)
    def _():
        for peer in line.values():
            pl.semaphore_signal(barrier, inc=1, device_id=peer, device_id_type=MESH)

    loads = [
        pltpu.make_async_copy(img_hbm, own.at[0], load_sem.at[0]),
        pltpu.make_async_copy(txt_hbm, own.at[1], load_sem.at[1]),
        pltpu.make_async_copy(weights_hbm, weights, load_sem.at[2]),
    ]
    for load in loads:
        load.start()
    for load in loads:
        load.wait()
    block = own[...].astype(jnp.float32).reshape(rows, width).astype(jnp.bfloat16)
    xj[0, core] = block
    xi[PEERS] = block
    pl.semaphore_wait(barrier, core * len(line) + 1 + PEERS)

    def hop(origin, step, c):
        src, dst = origin % NZ, (origin + step) % NZ
        lanes = slice(None) if dst != HALF else pl.ds(0 if step > 0 else half, half)
        return pltpu.make_async_remote_copy(
            src_ref=xj.at[src, c, :, lanes], dst_ref=xj.at[dst, c, :, lanes], send_sem=z_send, recv_sem=z_recv.at[group_of(origin, step, c)],
            device_id=line[step], device_id_type=MESH)

    hand = pltpu.make_async_remote_copy(
        src_ref=xj.at[0, core], dst_ref=xj.at[0, core], send_sem=hand_send, recv_sem=hand_recv,
        device_id=sibling, device_id_type=MESH)

    def across(slot):
        return pltpu.make_async_remote_copy(
            src_ref=xj.at[slot], dst_ref=xj.at[slot], send_sem=sib_send, recv_sem=sib_recv,
            device_id=sibling, device_id_type=MESH)

    def spread(k):
        return pltpu.make_async_remote_copy(
            src_ref=xi.at[PEERS], dst_ref=xi.at[k], send_sem=i_send, recv_sem=i_recv,
            device_id=ahead[k], device_id_type=MESH)

    def give(k):
        return pltpu.make_async_remote_copy(
            src_ref=part.at[k], dst_ref=inbox.at[k], send_sem=g_send, recv_sem=g_recv,
            device_id=behind[k], device_id_type=MESH)

    def landed(ref, sem):
        pltpu.make_async_copy(ref, ref, sem).wait()

    def begin(c):
        for origin, step in HOPS:
            if origin == 0:
                hop(0, step, c).start()

    pl.when(core == 1)(lambda: begin(1))
    hand.start()
    for k in range(PEERS):
        spread(k).start()
    hand.wait_recv()

    @pl.when(core == 1)
    def _():
        begin(0)
        for n, group in enumerate(ARRIVALS):
            landed(xj.at[0, pl.ds(0, 1)] if len(group) == 1 else xj.at[0] if sum(group[0][:2]) == HALF else xj.at[pl.ds(0, 2)], z_recv.at[n])
            for origin, step, c in group:
                here = origin + step
                for onward in HOPS:
                    if onward[0] == here:
                        hop(*onward, c).start()
                if c == 0 and abs(here) != HALF:
                    across(here % NZ).start()
        across(HALF).start()

    landed(xi.at[pl.ds(0, PEERS)], i_recv)
    pl.when(core == 0)(lambda: landed(xj.at[pl.ds(1, NZ - 1)], sib_recv))

    blocks = PEERS + 1
    keys = xj[...].reshape(2 * NZ * rows, width)
    scores = lax.dot_general(
        xi[...].reshape(blocks * rows, width), keys, (((1,), (1,)), ((), ())), preferred_element_type=jnp.float32)
    lanes = scores.shape[1]
    lane_kind = (lax.broadcasted_iota(jnp.int32, scores.shape, 1) // 8) % 2
    row_kind = (lax.broadcasted_iota(jnp.int32, scores.shape, 0) // 8) % 2
    turned = jnp.where(lane_kind == 0, pltpu.roll(scores, lanes - 8, 1), pltpu.roll(scores, 8, 1))
    turned = turned.reshape(blocks, 2, 8, lanes)
    turned = jnp.concatenate([turned[:, 1:], turned[:, :1]], axis=1).reshape(scores.shape)
    factor = jnp.where(lane_kind == row_kind, weights[1] * scale, weights[0] * scale)
    w[...] = ((scores - turned) * factor).astype(jnp.bfloat16)

    group = 4
    for first in range(0, blocks, group):
        total = jnp.dot(w[pl.ds(first * rows, group * rows), :], keys, preferred_element_type=jnp.float32)
        for k in range(first, first + group):
            block = total[(k - first) * rows : (k - first + 1) * rows]
            if k < PEERS:
                part[k] = block.astype(jnp.bfloat16)
                give(k).start()
            else:
                mine = block
    landed(inbox, g_recv)
    for k in range(PEERS):
        mine = mine + inbox[k].astype(jnp.float32)
    out[0] = mine[:8]
    out[1] = mine[8:]

    @pl.when(core == 1)
    def _():
        landed(xj.at[pl.ds(0, NZ - 1)], z_send)
        landed(xj.at[pl.ds(1, NZ - 1)], sib_send)

    hand.wait_send()
    landed(xi.at[pl.ds(0, PEERS)], i_send)
    landed(part, g_send)


def local(images, texts, loss_weights):
    count, width = images.shape
    batch = count * lax.axis_size("row") * lax.axis_size("col")
    scale = 1.0 / math.sqrt(width * batch)
    rows = 2 * count
    dma = pltpu.SemaphoreType.DMA
    grads = pl.pallas_call(
        functools.partial(kernel, scale),
        out_shape=pltpu.VMEM((2, count, width), jnp.float32),
        in_specs=[pl.BlockSpec(memory_space=pltpu.HBM)] * 3,
        out_specs=pl.BlockSpec(memory_space=pltpu.VMEM),
        scratch_shapes=[
            pltpu.SMEM((2,), jnp.float32),
            pltpu.VMEM((2, count, width), jnp.bfloat16),
            pltpu.VMEM((PEERS + 1, rows, width), jnp.bfloat16),
            pltpu.VMEM((NZ, CORES, rows, width), jnp.bfloat16),
            pltpu.VMEM(((PEERS + 1) * rows, 2 * NZ * rows), jnp.bfloat16),
            pltpu.VMEM((PEERS, rows, width), jnp.bfloat16),
            pltpu.VMEM((PEERS, rows, width), jnp.bfloat16),
            dma((3,)),
            dma, dma((len(ARRIVALS),)),
            dma, dma, dma, dma, dma, dma, dma, dma,
        ],
        compiler_params=pltpu.CompilerParams(collective_id=0, has_side_effects=True, vmem_limit_bytes=60 * 1024 * 1024),
    )(loss_weights, images, texts)
    return (grads[0], grads[1])


def solution(mesh):
    in_specs = (P(("row", "col"), None), P(("row", "col"), None), P())
    out_specs = (P(("row", "col"), None), P(("row", "col"), None))
    return jax.shard_map(local, mesh=mesh, in_specs=in_specs, out_specs=out_specs, check_vma=False)
```

```python
import functools
import math

import jax
import jax.numpy as jnp
from jax import lax
from jax.experimental import pallas as pl
from jax.experimental.pallas import tpu as pltpu
from jax.sharding import PartitionSpec as P

MESH = pl.DeviceIdType.MESH
NX, NY, NZ, CORES = 4, 4, 16, 2
HALF = NZ // 2
ROUNDS = NX // 2 + NY // 2 - 1


def ring_distance(step, size):
    return min(step, size - step)


PLANE = sorted(
    [(dx, dy) for dy in range(NY) for dx in range(NX)],
    key=lambda o: -(ring_distance(o[0], NX) + ring_distance(o[1], NY)),
)
PEERS = len(PLANE) - 1

NEAR = [(0, 3), (0, 1), (3, 2), (3, 1), (3, -1), (5, 3), (5, 2), (5, 1)]
HOPS = [hop for origin, step in NEAR for hop in ((origin, step), (-origin, -step))]
LINE_PEERS = sorted({step for _, step in HOPS})


def arrivals():
    level, order = {0: 0}, []
    for origin, step in NEAR:
        level[origin + step] = level[origin] + 1
    relays = [hop for hop in NEAR if any(origin == sum(hop) for origin, _ in NEAR)]
    for depth in sorted({level[sum(hop)] for hop in relays}):
        for c in (1, 0):
            for origin, step in relays:
                if level[origin + step] == depth:
                    order += [[(origin, step, c)], [(-origin, -step, c)]]
    for origin, step in sorted(set(NEAR) - set(relays), key=lambda hop: level[sum(hop)]):
        order.append([(origin, step, 1), (origin, step, 0), (-origin, -step, 1), (-origin, -step, 0)])
    return order


ARRIVALS = arrivals()


def group_of(origin, step, c):
    return next(n for n, group in enumerate(ARRIVALS) if (origin, step, c) in group)


def kernel(scale, weights_hbm, img_hbm, txt_hbm, out, weights, own, xi, xj, w, part, inbox, news, load_sem, z_send, z_recv, hand_send, hand_recv, sib_send, sib_recv, i_send, i_recv, g_send, g_recv):
    rows, width = xi.shape[1:]
    half = width // 2
    row, col = lax.axis_index("row"), lax.axis_index("col")
    y, zh, core = row // 4, (row // 2) % 2, row % 2
    zl, x = col // NX, col % NX
    z = zh * 8 + zl

    def device(x, y, z, core):
        return (y * 4 + (z // 8) * 2 + core, (z % 8) * NX + x)

    sibling = device(x, y, z, 1 - core)
    line = {d: device(x, y, (z + d + NZ) % NZ, core) for d in LINE_PEERS}
    ahead = [[device((x + dx) % NX, (y + dy) % NY, z, c) for dx, dy in PLANE[:PEERS]] for c in range(CORES)]
    beside = [[device((x + dx) % NX, (y + dy) % NY, z, c) for dx, dy in [(1, 0), (NX - 1, 0), (0, 1), (0, NY - 1)]] for c in range(CORES)]
    behind = [device((x + NX - dx) % NX, (y + NY - dy) % NY, z, core) for dx, dy in PLANE[:PEERS]]

    loads = [
        pltpu.make_async_copy(img_hbm, own.at[0], load_sem.at[0]),
        pltpu.make_async_copy(txt_hbm, own.at[1], load_sem.at[1]),
        pltpu.make_async_copy(weights_hbm, weights, load_sem.at[2]),
    ]
    for load in loads:
        load.start()

    barrier = pltpu.get_barrier_semaphore()
    for peer in [sibling] + beside[1]:
        pl.semaphore_signal(barrier, inc=1, device_id=peer, device_id_type=MESH)

    @pl.when(core == 1)
    def _():
        for peer in line.values():
            pl.semaphore_signal(barrier, inc=1, device_id=peer, device_id_type=MESH)

    for load in loads:
        load.wait()
    block = own[...].astype(jnp.float32).reshape(rows, width).astype(jnp.bfloat16)
    xj[0, core] = block
    xi[PEERS] = block
    pl.semaphore_wait(barrier, core * (len(line) + 2 * len(beside[1])) + 1)

    def hop(origin, step, c):
        src, dst = origin % NZ, (origin + step) % NZ
        lanes = slice(None) if dst != HALF else pl.ds(0 if step > 0 else half, half)
        return pltpu.make_async_remote_copy(
            src_ref=xj.at[src, c, :, lanes], dst_ref=xj.at[dst, c, :, lanes], send_sem=z_send, recv_sem=z_recv.at[group_of(origin, step, c)],
            device_id=line[step], device_id_type=MESH)

    hand = pltpu.make_async_remote_copy(
        src_ref=xj.at[0, core], dst_ref=xj.at[0, core], send_sem=hand_send, recv_sem=hand_recv,
        device_id=sibling, device_id_type=MESH)

    def across(slot):
        return pltpu.make_async_remote_copy(
            src_ref=xj.at[slot], dst_ref=xj.at[slot], send_sem=sib_send, recv_sem=sib_recv,
            device_id=sibling, device_id_type=MESH)

    def spread(k, c):
        return pltpu.make_async_remote_copy(
            src_ref=xj.at[0, c], dst_ref=xi.at[k], send_sem=i_send, recv_sem=i_recv,
            device_id=ahead[c][k], device_id_type=MESH)

    def give(k):
        return pltpu.make_async_remote_copy(
            src_ref=part.at[k], dst_ref=inbox.at[k], send_sem=g_send, recv_sem=g_recv,
            device_id=behind[k], device_id_type=MESH)

    def landed(ref, sem):
        pltpu.make_async_copy(ref, ref, sem).wait()

    def begin(c):
        for origin, step in HOPS:
            if origin == 0:
                hop(0, step, c).start()

    def spread_to(distance):
        for k, (dx, dy) in enumerate(PLANE[:PEERS]):
            if ring_distance(dx, NX) + ring_distance(dy, NY) == distance:
                for c in range(CORES):
                    spread(k, c).start()

    hand.start()
    pl.when(core == 1)(lambda: begin(1))
    hand.wait_recv()

    @pl.when(core == 0)
    def _():
        for n in range(ROUNDS + 1):
            if n > 0:
                pl.semaphore_wait(news.at[n - 1], len(beside[0]))
            if n < ROUNDS:
                for peer in beside[0]:
                    pl.semaphore_signal(news.at[n], inc=1, device_id=peer, device_id_type=MESH)
            spread_to(n + 1)

    @pl.when(core == 1)
    def _():
        begin(0)
        for n, group in enumerate(ARRIVALS):
            landed(xj.at[0, pl.ds(0, 1)] if len(group) == 1 else xj.at[0] if sum(group[0][:2]) == HALF else xj.at[pl.ds(0, 2)], z_recv.at[n])
            for origin, step, c in group:
                here = origin + step
                for onward in HOPS:
                    if onward[0] == here:
                        hop(*onward, c).start()
                if c == 0 and abs(here) != HALF:
                    across(here % NZ).start()
        across(HALF).start()

    landed(xi.at[pl.ds(0, PEERS)], i_recv)
    pl.when(core == 0)(lambda: landed(xj.at[pl.ds(1, NZ - 1)], sib_recv))

    blocks = PEERS + 1
    keys = xj[...].reshape(2 * NZ * rows, width)
    scores = lax.dot_general(
        xi[...].reshape(blocks * rows, width), keys, (((1,), (1,)), ((), ())), preferred_element_type=jnp.float32)
    lanes = scores.shape[1]
    lane_kind = (lax.broadcasted_iota(jnp.int32, scores.shape, 1) // 8) % 2
    row_kind = (lax.broadcasted_iota(jnp.int32, scores.shape, 0) // 8) % 2
    turned = jnp.where(lane_kind == 0, pltpu.roll(scores, lanes - 8, 1), pltpu.roll(scores, 8, 1))
    turned = turned.reshape(blocks, 2, 8, lanes)
    turned = jnp.concatenate([turned[:, 1:], turned[:, :1]], axis=1).reshape(scores.shape)
    factor = jnp.where(lane_kind == row_kind, weights[1] * scale, weights[0] * scale)
    w[...] = ((scores - turned) * factor).astype(jnp.bfloat16)

    group = 4
    for first in range(0, blocks, group):
        total = jnp.dot(w[pl.ds(first * rows, group * rows), :], keys, preferred_element_type=jnp.float32)
        for k in range(first, first + group):
            block = total[(k - first) * rows : (k - first + 1) * rows]
            if k < PEERS:
                part[k] = block.astype(jnp.bfloat16)
                give(k).start()
            else:
                mine = block
    landed(inbox, g_recv)
    for k in range(PEERS):
        mine = mine + inbox[k].astype(jnp.float32)
    out[0] = mine[:8]
    out[1] = mine[8:]

    @pl.when(core == 1)
    def _():
        landed(xj.at[pl.ds(0, NZ - 1)], z_send)
        landed(xj.at[pl.ds(1, NZ - 1)], sib_send)

    hand.wait_send()

    @pl.when(core == 0)
    def _():
        landed(xj.at[pl.ds(0, PEERS)], i_send)

    landed(part, g_send)


def local(images, texts, loss_weights):
    count, width = images.shape
    batch = count * lax.axis_size("row") * lax.axis_size("col")
    scale = 1.0 / math.sqrt(width * batch)
    rows = 2 * count
    dma = pltpu.SemaphoreType.DMA
    grads = pl.pallas_call(
        functools.partial(kernel, scale),
        out_shape=pltpu.VMEM((2, count, width), jnp.float32),
        in_specs=[pl.BlockSpec(memory_space=pltpu.HBM)] * 3,
        out_specs=pl.BlockSpec(memory_space=pltpu.VMEM),
        scratch_shapes=[
            pltpu.SMEM((2,), jnp.float32),
            pltpu.VMEM((2, count, width), jnp.bfloat16),
            pltpu.VMEM((PEERS + 1, rows, width), jnp.bfloat16),
            pltpu.VMEM((NZ, CORES, rows, width), jnp.bfloat16),
            pltpu.VMEM(((PEERS + 1) * rows, 2 * NZ * rows), jnp.bfloat16),
            pltpu.VMEM((PEERS, rows, width), jnp.bfloat16),
            pltpu.VMEM((PEERS, rows, width), jnp.bfloat16),
            pltpu.SemaphoreType.REGULAR((ROUNDS,)),
            dma((3,)),
            dma, dma((len(ARRIVALS),)),
            dma, dma, dma, dma, dma, dma, dma, dma,
        ],
        compiler_params=pltpu.CompilerParams(collective_id=0, has_side_effects=True, vmem_limit_bytes=60 * 1024 * 1024),
    )(loss_weights, images, texts)
    return (grads[0], grads[1])


def solution(mesh):
    in_specs = (P(("row", "col"), None), P(("row", "col"), None), P())
    out_specs = (P(("row", "col"), None), P(("row", "col"), None))
    return jax.shard_map(local, mesh=mesh, in_specs=in_specs, out_specs=out_specs, check_vma=False)
```

```python
import functools
import math

import jax
import jax.numpy as jnp
from jax import lax
from jax.experimental import pallas as pl
from jax.experimental.pallas import tpu as pltpu
from jax.sharding import PartitionSpec as P

MESH = pl.DeviceIdType.MESH
NX, NY, NZ, CORES = 4, 4, 16, 2
HALF = NZ // 2


def ring_distance(step, size):
    return min(step, size - step)


PLANE = sorted(
    [(dx, dy) for dy in range(NY) for dx in range(NX)],
    key=lambda o: -(ring_distance(o[0], NX) + ring_distance(o[1], NY)),
)
PEERS = len(PLANE) - 1


def at_distance(distance):
    return [k for k, (dx, dy) in enumerate(PLANE) if ring_distance(dx, NX) + ring_distance(dy, NY) == distance]


NEAR = [(0, 3), (0, 1), (3, 3), (3, -1), (3, 1), (6, 2), (6, 1), (6, -1)]
HOPS = [hop for origin, step in NEAR for hop in ((origin, step), (-origin, -step))]
LINE_PEERS = sorted({step for _, step in HOPS})


def arrivals():
    level, order = {0: 0}, []
    for origin, step in NEAR:
        level[origin + step] = level[origin] + 1
    relays = [hop for hop in NEAR if any(origin == sum(hop) for origin, _ in NEAR)]
    for depth in sorted({level[sum(hop)] for hop in relays}):
        for c in (1, 0):
            for origin, step in relays:
                if level[origin + step] == depth:
                    order += [[(origin, step, c)], [(-origin, -step, c)]]
    for origin, step in sorted(set(NEAR) - set(relays), key=lambda hop: level[sum(hop)]):
        order.append([(origin, step, 1), (origin, step, 0), (-origin, -step, 1), (-origin, -step, 0)])
    return order


ARRIVALS = arrivals()


def urgent(hop):
    last = max(NEAR, key=lambda other: abs(sum(other)))[0]
    up = hop if hop in NEAR else (-hop[0], -hop[1])
    return any(origin == sum(up) for origin, _ in NEAR) or up[0] == last


def group_of(origin, step, c):
    return next(n for n, group in enumerate(ARRIVALS) if (origin, step, c) in group)


def kernel(scale, weights_hbm, img_hbm, txt_hbm, out, weights, own, xi, xj, w, part, inbox, news, load_sem, z_send, z_recv, hand_send, hand_recv, sib_send, sib_recv, i_send, i_recv, g_send, g_recv):
    rows, width = xi.shape[1:]
    half = width // 2
    row, col = lax.axis_index("row"), lax.axis_index("col")
    y, zh, core = row // 4, (row // 2) % 2, row % 2
    zl, x = col // NX, col % NX
    z = zh * 8 + zl

    def device(x, y, z, core):
        return (y * 4 + (z // 8) * 2 + core, (z % 8) * NX + x)

    sibling = device(x, y, z, 1 - core)
    line = {d: device(x, y, (z + d + NZ) % NZ, core) for d in LINE_PEERS}
    ahead = [[device((x + dx) % NX, (y + dy) % NY, z, c) for dx, dy in PLANE[:PEERS]] for c in range(CORES)]
    beside = [[device((x + dx) % NX, (y + dy) % NY, z, c) for dx, dy in [(1, 0), (NX - 1, 0), (0, 1), (0, NY - 1)]] for c in range(CORES)]
    behind = [device((x + NX - dx) % NX, (y + NY - dy) % NY, z, core) for dx, dy in PLANE[:PEERS]]

    loads = [
        pltpu.make_async_copy(img_hbm, own.at[0], load_sem.at[0]),
        pltpu.make_async_copy(txt_hbm, own.at[1], load_sem.at[1]),
        pltpu.make_async_copy(weights_hbm, weights, load_sem.at[2]),
    ]
    for load in loads:
        load.start()

    barrier = pltpu.get_barrier_semaphore()
    for peer in [sibling] + beside[1]:
        pl.semaphore_signal(barrier, inc=1, device_id=peer, device_id_type=MESH)

    @pl.when(core == 1)
    def _():
        for peer in line.values():
            pl.semaphore_signal(barrier, inc=1, device_id=peer, device_id_type=MESH)

    for load in loads:
        load.wait()
    block = own[...].astype(jnp.float32).reshape(rows, width).astype(jnp.bfloat16)
    xj[0, core] = block
    xi[PEERS] = block
    pl.semaphore_wait(barrier, core * (len(line) + 2 * len(beside[1])) + 1)

    def hop(origin, step, c):
        src, dst = origin % NZ, (origin + step) % NZ
        lanes = slice(None) if dst != HALF else pl.ds(0 if step > 0 else half, half)
        return pltpu.make_async_remote_copy(
            src_ref=xj.at[src, c, :, lanes], dst_ref=xj.at[dst, c, :, lanes], send_sem=z_send, recv_sem=z_recv.at[group_of(origin, step, c)],
            device_id=line[step], device_id_type=MESH)

    hand = pltpu.make_async_remote_copy(
        src_ref=xj.at[0, core], dst_ref=xj.at[0, core], send_sem=hand_send, recv_sem=hand_recv,
        device_id=sibling, device_id_type=MESH)

    def across(slot):
        return pltpu.make_async_remote_copy(
            src_ref=xj.at[slot], dst_ref=xj.at[slot], send_sem=sib_send, recv_sem=sib_recv,
            device_id=sibling, device_id_type=MESH)

    def spread(k, c):
        return pltpu.make_async_remote_copy(
            src_ref=xj.at[0, c], dst_ref=xi.at[k], send_sem=i_send, recv_sem=i_recv,
            device_id=ahead[c][k], device_id_type=MESH)

    def give(k):
        return pltpu.make_async_remote_copy(
            src_ref=part.at[k], dst_ref=inbox.at[k], send_sem=g_send, recv_sem=g_recv,
            device_id=behind[k], device_id_type=MESH)

    def landed(ref, sem):
        pltpu.make_async_copy(ref, ref, sem).wait()

    def start(here, c, first):
        for onward in HOPS:
            if onward[0] == here and urgent(onward) == first:
                hop(*onward, c).start()

    second = at_distance(2)

    def spread_to(distance):
        for k in at_distance(distance):
            for c in range(CORES):
                spread(k, c).start()

    hand.start()

    @pl.when(core == 1)
    def _():
        for peer in beside[0]:
            pl.semaphore_signal(news.at[0], inc=1, device_id=peer, device_id_type=MESH)
        start(0, 1, True)

    hand.wait_recv()

    @pl.when(core == 0)
    def _():
        spread_to(1)
        pl.semaphore_wait(news.at[0], len(beside[0]))
        for k in second:
            pl.semaphore_signal(news.at[1], inc=1, device_id=ahead[0][k], device_id_type=MESH)
        spread_to(2)
        pl.semaphore_wait(news.at[1], len(second))
        spread_to(4)
        spread_to(3)

    @pl.when(core == 1)
    def _():
        start(0, 0, True)
        start(0, 1, False)
        start(0, 0, False)
        left = []
        for n, group in enumerate(ARRIVALS):
            landed(xj.at[0, pl.ds(0, 1)] if len(group) == 1 else xj.at[0] if sum(group[0][:2]) == HALF else xj.at[pl.ds(0, 2)], z_recv.at[n])
            for origin, step, c in group:
                here = origin + step
                start(here, c, True)
                left.append((here, c))
                if c == 0 and abs(here) != HALF:
                    across(here % NZ).start()
            if len(group) == 1 and group[0][1] < 0 and group[0][2] == 0:
                for here, c in left:
                    start(here, c, False)
                left = []
        across(HALF).start()

    landed(xi.at[pl.ds(0, PEERS)], i_recv)
    pl.when(core == 0)(lambda: landed(xj.at[pl.ds(1, NZ - 1)], sib_recv))

    blocks = PEERS + 1
    keys = xj[...].reshape(2 * NZ * rows, width)
    scores = lax.dot_general(
        xi[...].reshape(blocks * rows, width), keys, (((1,), (1,)), ((), ())), preferred_element_type=jnp.float32)
    lanes = scores.shape[1]
    lane_kind = (lax.broadcasted_iota(jnp.int32, scores.shape, 1) // 8) % 2
    row_kind = (lax.broadcasted_iota(jnp.int32, scores.shape, 0) // 8) % 2
    turned = jnp.where(lane_kind == 0, pltpu.roll(scores, lanes - 8, 1), pltpu.roll(scores, 8, 1))
    turned = turned.reshape(blocks, 2, 8, lanes)
    turned = jnp.concatenate([turned[:, 1:], turned[:, :1]], axis=1).reshape(scores.shape)
    factor = jnp.where(lane_kind == row_kind, weights[1] * scale, weights[0] * scale)
    w[...] = ((scores - turned) * factor).astype(jnp.bfloat16)

    group = 4
    for first in range(0, blocks, group):
        total = jnp.dot(w[pl.ds(first * rows, group * rows), :], keys, preferred_element_type=jnp.float32)
        for k in range(first, first + group):
            block = total[(k - first) * rows : (k - first + 1) * rows]
            if k < PEERS:
                part[k] = block.astype(jnp.bfloat16)
                give(k).start()
            else:
                mine = block
    landed(inbox, g_recv)
    for k in range(PEERS):
        mine = mine + inbox[k].astype(jnp.float32)
    out[0] = mine[:8]
    out[1] = mine[8:]

    @pl.when(core == 1)
    def _():
        landed(xj.at[pl.ds(0, NZ - 1)], z_send)
        landed(xj.at[pl.ds(1, NZ - 1)], sib_send)

    hand.wait_send()

    @pl.when(core == 0)
    def _():
        landed(xj.at[pl.ds(0, PEERS)], i_send)

    landed(part, g_send)


def local(images, texts, loss_weights):
    count, width = images.shape
    batch = count * lax.axis_size("row") * lax.axis_size("col")
    scale = 1.0 / math.sqrt(width * batch)
    rows = 2 * count
    dma = pltpu.SemaphoreType.DMA
    grads = pl.pallas_call(
        functools.partial(kernel, scale),
        out_shape=pltpu.VMEM((2, count, width), jnp.float32),
        in_specs=[pl.BlockSpec(memory_space=pltpu.HBM)] * 3,
        out_specs=pl.BlockSpec(memory_space=pltpu.VMEM),
        scratch_shapes=[
            pltpu.SMEM((2,), jnp.float32),
            pltpu.VMEM((2, count, width), jnp.bfloat16),
            pltpu.VMEM((PEERS + 1, rows, width), jnp.bfloat16),
            pltpu.VMEM((NZ, CORES, rows, width), jnp.bfloat16),
            pltpu.VMEM(((PEERS + 1) * rows, 2 * NZ * rows), jnp.bfloat16),
            pltpu.VMEM((PEERS, rows, width), jnp.bfloat16),
            pltpu.VMEM((PEERS, rows, width), jnp.bfloat16),
            pltpu.SemaphoreType.REGULAR((2,)),
            dma((3,)),
            dma, dma((len(ARRIVALS),)),
            dma, dma, dma, dma, dma, dma, dma, dma,
        ],
        compiler_params=pltpu.CompilerParams(collective_id=0, has_side_effects=True, vmem_limit_bytes=60 * 1024 * 1024),
    )(loss_weights, images, texts)
    return (grads[0], grads[1])


def solution(mesh):
    in_specs = (P(("row", "col"), None), P(("row", "col"), None), P())
    out_specs = (P(("row", "col"), None), P(("row", "col"), None))
    return jax.shard_map(local, mesh=mesh, in_specs=in_specs, out_specs=out_specs, check_vma=False)
```

```python
import functools
import math

import jax
import jax.numpy as jnp
from jax import lax
from jax.experimental import pallas as pl
from jax.experimental.pallas import tpu as pltpu
from jax.sharding import PartitionSpec as P

MESH = pl.DeviceIdType.MESH
NX, NY, NZ, CORES = 4, 4, 16, 2
HALF = NZ // 2


def ring_distance(step, size):
    return min(step, size - step)


PLANE = sorted(
    [(dx, dy) for dy in range(NY) for dx in range(NX)],
    key=lambda o: -(ring_distance(o[0], NX) + ring_distance(o[1], NY)),
)
PEERS = len(PLANE) - 1
SHARE = 5


def at_distance(distance):
    return [k for k, (dx, dy) in enumerate(PLANE) if ring_distance(dx, NX) + ring_distance(dy, NY) == distance]


NEAR = [(0, 3), (0, 1), (3, 3), (3, -1), (3, 1), (6, 2), (6, 1), (6, -1)]
HOPS = [hop for origin, step in NEAR for hop in ((origin, step), (-origin, -step))]
LINE_PEERS = sorted({step for _, step in HOPS})


def arrivals():
    level, order = {0: 0}, []
    for origin, step in NEAR:
        level[origin + step] = level[origin] + 1
    relays = [hop for hop in NEAR if any(origin == sum(hop) for origin, _ in NEAR)]
    for depth in sorted({level[sum(hop)] for hop in relays}):
        for c in (1, 0):
            for origin, step in relays:
                if level[origin + step] == depth:
                    order += [[(origin, step, c)], [(-origin, -step, c)]]
    for origin, step in sorted(set(NEAR) - set(relays), key=lambda hop: level[sum(hop)]):
        order.append([(origin, step, 1), (origin, step, 0), (-origin, -step, 1), (-origin, -step, 0)])
    return order


ARRIVALS = arrivals()


def urgent(hop):
    last = max(NEAR, key=lambda other: abs(sum(other)))[0]
    up = hop if hop in NEAR else (-hop[0], -hop[1])
    return any(origin == sum(up) for origin, _ in NEAR) or up[0] == last


def group_of(origin, step, c):
    return next(n for n, group in enumerate(ARRIVALS) if (origin, step, c) in group)


def kernel(scale, weights_hbm, img_hbm, txt_hbm, out, weights, own, xi, xj, part, inbox, news, load_sem, z_send, z_recv, hand_send, hand_recv, sib_send, sib_recv, i_send, i_recv, g_send, g_recv):
    rows, width = xi.shape[1:]
    half = width // 2
    row, col = lax.axis_index("row"), lax.axis_index("col")
    y, zh, core = row // 4, (row // 2) % 2, row % 2
    zl, x = col // NX, col % NX
    z = zh * 8 + zl

    def device(x, y, z, core):
        return (y * 4 + (z // 8) * 2 + core, (z % 8) * NX + x)

    sibling = device(x, y, z, 1 - core)
    line = {d: device(x, y, (z + d + NZ) % NZ, core) for d in LINE_PEERS}
    ahead = [[device((x + dx) % NX, (y + dy) % NY, z, c) for dx, dy in PLANE[:PEERS]] for c in range(CORES)]
    beside = [[device((x + dx) % NX, (y + dy) % NY, z, c) for dx, dy in [(1, 0), (NX - 1, 0), (0, 1), (0, NY - 1)]] for c in range(CORES)]
    behind = [device((x + NX - dx) % NX, (y + NY - dy) % NY, z, core) for dx, dy in PLANE[:PEERS]]

    loads = [
        pltpu.make_async_copy(img_hbm, own.at[0], load_sem.at[0]),
        pltpu.make_async_copy(txt_hbm, own.at[1], load_sem.at[1]),
        pltpu.make_async_copy(weights_hbm, weights, load_sem.at[2]),
    ]
    for load in loads:
        load.start()

    barrier = pltpu.get_barrier_semaphore()
    for peer in [sibling] + beside[1]:
        pl.semaphore_signal(barrier, inc=1, device_id=peer, device_id_type=MESH)

    @pl.when(core == 1)
    def _():
        for peer in line.values():
            pl.semaphore_signal(barrier, inc=1, device_id=peer, device_id_type=MESH)

    for load in loads:
        load.wait()
    block = own[...].astype(jnp.float32).reshape(rows, width).astype(jnp.bfloat16)
    xj[0, core] = block
    xi[PEERS] = block
    pl.semaphore_wait(barrier, core * (len(line) + 2 * len(beside[1])) + 1)

    def hop(origin, step, c):
        src, dst = origin % NZ, (origin + step) % NZ
        lanes = slice(None) if dst != HALF else pl.ds(0 if step > 0 else half, half)
        return pltpu.make_async_remote_copy(
            src_ref=xj.at[src, c, :, lanes], dst_ref=xj.at[dst, c, :, lanes], send_sem=z_send, recv_sem=z_recv.at[group_of(origin, step, c)],
            device_id=line[step], device_id_type=MESH)

    hand = pltpu.make_async_remote_copy(
        src_ref=xj.at[0, core], dst_ref=xj.at[0, core], send_sem=hand_send, recv_sem=hand_recv,
        device_id=sibling, device_id_type=MESH)

    def across(slot):
        return pltpu.make_async_remote_copy(
            src_ref=xj.at[slot], dst_ref=xj.at[slot], send_sem=sib_send, recv_sem=sib_recv,
            device_id=sibling, device_id_type=MESH)

    def spread(k, c):
        return pltpu.make_async_remote_copy(
            src_ref=xj.at[0, c], dst_ref=xi.at[k], send_sem=i_send, recv_sem=i_recv,
            device_id=ahead[c][k], device_id_type=MESH)

    def give(k):
        return pltpu.make_async_remote_copy(
            src_ref=part.at[k], dst_ref=inbox.at[k], send_sem=g_send, recv_sem=g_recv.at[k // SHARE],
            device_id=behind[k], device_id_type=MESH)

    def landed(ref, sem):
        pltpu.make_async_copy(ref, ref, sem).wait()

    def start(here, c, first):
        for onward in HOPS:
            if onward[0] == here and urgent(onward) == first:
                hop(*onward, c).start()

    second = at_distance(2)

    def spread_to(distance):
        for k in at_distance(distance):
            for c in range(CORES):
                spread(k, c).start()

    hand.start()

    @pl.when(core == 1)
    def _():
        for peer in beside[0]:
            pl.semaphore_signal(news.at[0], inc=1, device_id=peer, device_id_type=MESH)
        start(0, 1, True)

    hand.wait_recv()

    @pl.when(core == 0)
    def _():
        spread_to(1)
        pl.semaphore_wait(news.at[0], len(beside[0]))
        for k in second:
            pl.semaphore_signal(news.at[1], inc=1, device_id=ahead[0][k], device_id_type=MESH)
        spread_to(2)
        pl.semaphore_wait(news.at[1], len(second))
        spread_to(4)
        spread_to(3)

    @pl.when(core == 1)
    def _():
        start(0, 0, True)
        start(0, 1, False)
        start(0, 0, False)
        left = []
        for n, group in enumerate(ARRIVALS):
            landed(xj.at[0, pl.ds(0, 1)] if len(group) == 1 else xj.at[0] if sum(group[0][:2]) == HALF else xj.at[pl.ds(0, 2)], z_recv.at[n])
            for origin, step, c in group:
                here = origin + step
                start(here, c, True)
                left.append((here, c))
                if c == 0 and abs(here) != HALF:
                    across(here % NZ).start()
            if len(group) == 1 and group[0][1] < 0 and group[0][2] == 0:
                for here, c in left:
                    start(here, c, False)
                left = []
        across(HALF).start()

    landed(xi.at[pl.ds(0, PEERS)], i_recv)
    pl.when(core == 0)(lambda: landed(xj.at[pl.ds(1, NZ - 1)], sib_recv))

    keys = xj[...].reshape(2 * NZ * rows, width)
    first = 0
    for size in (8, 8):
        scores = lax.dot_general(
            xi[pl.ds(first, size)].reshape(size * rows, width), keys, (((1,), (1,)), ((), ())), preferred_element_type=jnp.float32)
        lanes = scores.shape[1]
        lane_kind = (lax.broadcasted_iota(jnp.int32, scores.shape, 1) // 8) % 2
        row_kind = (lax.broadcasted_iota(jnp.int32, scores.shape, 0) // 8) % 2
        turned = jnp.where(lane_kind == 0, pltpu.roll(scores, lanes - 8, 1), pltpu.roll(scores, 8, 1))
        turned = turned.reshape(size, 2, 8, lanes)
        turned = jnp.concatenate([turned[:, 1:], turned[:, :1]], axis=1).reshape(scores.shape)
        factor = jnp.where(lane_kind == row_kind, weights[1] * scale, weights[0] * scale)
        w = ((scores - turned) * factor).astype(jnp.bfloat16)
        total = jnp.dot(w, keys, preferred_element_type=jnp.float32)
        for k in range(first, first + size):
            block = total[(k - first) * rows : (k - first + 1) * rows]
            if k < PEERS:
                part[k] = block.astype(jnp.bfloat16)
                give(k).start()
            else:
                mine = block
        first += size
    for first in range(0, PEERS, SHARE):
        landed(inbox.at[pl.ds(first, SHARE)], g_recv.at[first // SHARE])
        for k in range(first, first + SHARE):
            mine = mine + inbox[k].astype(jnp.float32)
    out[0] = mine[:8]
    out[1] = mine[8:]

    @pl.when(core == 1)
    def _():
        landed(xj.at[pl.ds(0, NZ - 1)], z_send)
        landed(xj.at[pl.ds(1, NZ - 1)], sib_send)

    hand.wait_send()

    @pl.when(core == 0)
    def _():
        landed(xj.at[pl.ds(0, PEERS)], i_send)

    landed(part, g_send)


def local(images, texts, loss_weights):
    count, width = images.shape
    batch = count * lax.axis_size("row") * lax.axis_size("col")
    scale = 1.0 / math.sqrt(width * batch)
    rows = 2 * count
    dma = pltpu.SemaphoreType.DMA
    grads = pl.pallas_call(
        functools.partial(kernel, scale),
        out_shape=pltpu.VMEM((2, count, width), jnp.float32),
        in_specs=[pl.BlockSpec(memory_space=pltpu.HBM)] * 3,
        out_specs=pl.BlockSpec(memory_space=pltpu.VMEM),
        scratch_shapes=[
            pltpu.SMEM((2,), jnp.float32),
            pltpu.VMEM((2, count, width), jnp.bfloat16),
            pltpu.VMEM((PEERS + 1, rows, width), jnp.bfloat16),
            pltpu.VMEM((NZ, CORES, rows, width), jnp.bfloat16),
            pltpu.VMEM((PEERS, rows, width), jnp.bfloat16),
            pltpu.VMEM((PEERS, rows, width), jnp.bfloat16),
            pltpu.SemaphoreType.REGULAR((2,)),
            dma((3,)),
            dma, dma((len(ARRIVALS),)),
            dma, dma, dma, dma, dma, dma, dma, dma((PEERS // SHARE,)),
        ],
        compiler_params=pltpu.CompilerParams(collective_id=0, has_side_effects=True, vmem_limit_bytes=60 * 1024 * 1024),
    )(loss_weights, images, texts)
    return (grads[0], grads[1])


def solution(mesh):
    in_specs = (P(("row", "col"), None), P(("row", "col"), None), P())
    out_specs = (P(("row", "col"), None), P(("row", "col"), None))
    return jax.shard_map(local, mesh=mesh, in_specs=in_specs, out_specs=out_specs, check_vma=False)
```

```python
import functools
import math

import jax
import jax.numpy as jnp
from jax import lax
from jax.experimental import pallas as pl
from jax.experimental.pallas import tpu as pltpu
from jax.sharding import PartitionSpec as P

MESH = pl.DeviceIdType.MESH
NX, NY, NZ, CORES = 4, 4, 16, 2
HALF = NZ // 2


def ring_distance(step, size):
    return min(step, size - step)


PLANE = sorted(
    [(dx, dy) for dy in range(NY) for dx in range(NX)],
    key=lambda o: -(ring_distance(o[0], NX) + ring_distance(o[1], NY)),
)
PEERS = len(PLANE) - 1
SHARE = 5


def at_distance(distance):
    return [k for k, (dx, dy) in enumerate(PLANE) if ring_distance(dx, NX) + ring_distance(dy, NY) == distance]


NEAR = [(0, 3), (0, 1), (3, 3), (3, -1), (3, 1), (6, 2), (6, 1), (6, -1)]
HOPS = [hop for origin, step in NEAR for hop in ((origin, step), (-origin, -step))]
LINE_PEERS = sorted({step for _, step in HOPS})


def arrivals():
    level, order = {0: 0}, []
    for origin, step in NEAR:
        level[origin + step] = level[origin] + 1
    relays = [hop for hop in NEAR if any(origin == sum(hop) for origin, _ in NEAR)]
    for depth in sorted({level[sum(hop)] for hop in relays}):
        for c in (1, 0):
            for origin, step in relays:
                if level[origin + step] == depth:
                    order += [[(origin, step, c)], [(-origin, -step, c)]]
    for origin, step in sorted(set(NEAR) - set(relays), key=lambda hop: level[sum(hop)]):
        order.append([(origin, step, 1), (origin, step, 0), (-origin, -step, 1), (-origin, -step, 0)])
    return order


ARRIVALS = arrivals()


def urgent(hop):
    last = max(NEAR, key=lambda other: abs(sum(other)))[0]
    up = hop if hop in NEAR else (-hop[0], -hop[1])
    return any(origin == sum(up) for origin, _ in NEAR) or up[0] == last


def group_of(origin, step, c):
    return next(n for n, group in enumerate(ARRIVALS) if (origin, step, c) in group)


def kernel(scale, weights_hbm, img_hbm, txt_hbm, out, weights, own, xi, xj, w, part, inbox, news, load_sem, z_send, z_recv, hand_send, hand_recv, sib_send, sib_recv, i_send, i_recv, g_send, g_recv):
    rows, width = xi.shape[1:]
    half = width // 2
    row, col = lax.axis_index("row"), lax.axis_index("col")
    y, zh, core = row // 4, (row // 2) % 2, row % 2
    zl, x = col // NX, col % NX
    z = zh * 8 + zl

    def device(x, y, z, core):
        return (y * 4 + (z // 8) * 2 + core, (z % 8) * NX + x)

    sibling = device(x, y, z, 1 - core)
    line = {d: device(x, y, (z + d + NZ) % NZ, core) for d in LINE_PEERS}
    ahead = [[device((x + dx) % NX, (y + dy) % NY, z, c) for dx, dy in PLANE[:PEERS]] for c in range(CORES)]
    beside = [[device((x + dx) % NX, (y + dy) % NY, z, c) for dx, dy in [(1, 0), (NX - 1, 0), (0, 1), (0, NY - 1)]] for c in range(CORES)]
    behind = [device((x + NX - dx) % NX, (y + NY - dy) % NY, z, core) for dx, dy in PLANE[:PEERS]]

    loads = [
        pltpu.make_async_copy(img_hbm, own.at[0], load_sem.at[0]),
        pltpu.make_async_copy(txt_hbm, own.at[1], load_sem.at[1]),
        pltpu.make_async_copy(weights_hbm, weights, load_sem.at[2]),
    ]
    for load in loads:
        load.start()

    barrier = pltpu.get_barrier_semaphore()
    @pl.when(core == 1)
    def _():
        for peer in line.values():
            pl.semaphore_signal(barrier, inc=1, device_id=peer, device_id_type=MESH)

    for peer in [sibling] + beside[1]:
        pl.semaphore_signal(barrier, inc=1, device_id=peer, device_id_type=MESH)

    for load in loads:
        load.wait()
    block = own[...].astype(jnp.float32).reshape(rows, width).astype(jnp.bfloat16)
    xj[0, core] = block
    xi[PEERS] = block
    pl.semaphore_wait(barrier, core * (len(line) + 2 * len(beside[1])) + 1)

    def hop(origin, step, c):
        src, dst = origin % NZ, (origin + step) % NZ
        lanes = slice(None) if dst != HALF else pl.ds(0 if step > 0 else half, half)
        return pltpu.make_async_remote_copy(
            src_ref=xj.at[src, c, :, lanes], dst_ref=xj.at[dst, c, :, lanes], send_sem=z_send, recv_sem=z_recv.at[group_of(origin, step, c)],
            device_id=line[step], device_id_type=MESH)

    hand = pltpu.make_async_remote_copy(
        src_ref=xj.at[0, core], dst_ref=xj.at[0, core], send_sem=hand_send, recv_sem=hand_recv,
        device_id=sibling, device_id_type=MESH)

    def across(slot):
        return pltpu.make_async_remote_copy(
            src_ref=xj.at[slot], dst_ref=xj.at[slot], send_sem=sib_send, recv_sem=sib_recv,
            device_id=sibling, device_id_type=MESH)

    def spread(k, c):
        return pltpu.make_async_remote_copy(
            src_ref=xj.at[0, c], dst_ref=xi.at[k], send_sem=i_send, recv_sem=i_recv,
            device_id=ahead[c][k], device_id_type=MESH)

    def give(k):
        return pltpu.make_async_remote_copy(
            src_ref=part.at[k], dst_ref=inbox.at[k], send_sem=g_send, recv_sem=g_recv.at[k // SHARE],
            device_id=behind[k], device_id_type=MESH)

    def landed(ref, sem):
        pltpu.make_async_copy(ref, ref, sem).wait()

    def start(here, c, first):
        for onward in HOPS:
            if onward[0] == here and urgent(onward) == first:
                hop(*onward, c).start()

    second = at_distance(2)

    def spread_to(distance):
        for k in at_distance(distance):
            for c in range(CORES):
                spread(k, c).start()

    hand.start()

    @pl.when(core == 1)
    def _():
        for peer in beside[0]:
            pl.semaphore_signal(news.at[0], inc=1, device_id=peer, device_id_type=MESH)
        start(0, 1, True)

    hand.wait_recv()

    @pl.when(core == 0)
    def _():
        spread_to(1)
        pl.semaphore_wait(news.at[0], len(beside[0]))
        for k in second:
            pl.semaphore_signal(news.at[1], inc=1, device_id=ahead[0][k], device_id_type=MESH)
        spread_to(2)
        pl.semaphore_wait(news.at[1], len(second))
        spread_to(4)
        spread_to(3)

    @pl.when(core == 1)
    def _():
        start(0, 0, True)
        start(0, 1, False)
        start(0, 0, False)
        left = []
        for n, group in enumerate(ARRIVALS):
            landed(xj.at[0, pl.ds(0, 1)] if len(group) == 1 else xj.at[0] if sum(group[0][:2]) == HALF else xj.at[pl.ds(0, 2)], z_recv.at[n])
            for origin, step, c in group:
                here = origin + step
                start(here, c, True)
                left.append((here, c))
                if c == 0 and abs(here) != HALF:
                    across(here % NZ).start()
            if len(group) == 1 and group[0][1] < 0 and group[0][2] == 0:
                for here, c in left:
                    start(here, c, False)
                left = []
        across(HALF).start()

    landed(xi.at[pl.ds(0, PEERS)], i_recv)
    pl.when(core == 0)(lambda: landed(xj.at[pl.ds(1, NZ - 1)], sib_recv))

    blocks = PEERS + 1
    keys = xj[...].reshape(2 * NZ * rows, width)
    scores = lax.dot_general(
        xi[...].reshape(blocks * rows, width), keys, (((1,), (1,)), ((), ())), preferred_element_type=jnp.float32)
    lanes = scores.shape[1]
    lane_kind = (lax.broadcasted_iota(jnp.int32, scores.shape, 1) // 8) % 2
    row_kind = (lax.broadcasted_iota(jnp.int32, scores.shape, 0) // 8) % 2
    turned = jnp.where(lane_kind == 0, pltpu.roll(scores, lanes - 8, 1), pltpu.roll(scores, 8, 1))
    turned = turned.reshape(blocks, 2, 8, lanes)
    turned = jnp.concatenate([turned[:, 1:], turned[:, :1]], axis=1).reshape(scores.shape)
    factor = jnp.where(lane_kind == row_kind, weights[1] * scale, weights[0] * scale)
    w[...] = ((scores - turned) * factor).astype(jnp.bfloat16)

    group = 4
    for first in range(0, blocks, group):
        total = jnp.dot(w[pl.ds(first * rows, group * rows), :], keys, preferred_element_type=jnp.float32)
        for k in range(first, first + group):
            block = total[(k - first) * rows : (k - first + 1) * rows]
            if k < PEERS:
                part[k] = block.astype(jnp.bfloat16)
                give(k).start()
            else:
                mine = block
    for first in range(0, PEERS, SHARE):
        landed(inbox.at[pl.ds(first, SHARE)], g_recv.at[first // SHARE])
        for k in range(first, first + SHARE):
            mine = mine + inbox[k].astype(jnp.float32)
    out[0] = mine[:8]
    out[1] = mine[8:]

    @pl.when(core == 1)
    def _():
        landed(xj.at[pl.ds(0, NZ - 1)], z_send)
        landed(xj.at[pl.ds(1, NZ - 1)], sib_send)

    hand.wait_send()

    @pl.when(core == 0)
    def _():
        landed(xj.at[pl.ds(0, PEERS)], i_send)

    landed(part, g_send)


def local(images, texts, loss_weights):
    count, width = images.shape
    batch = count * lax.axis_size("row") * lax.axis_size("col")
    scale = 1.0 / math.sqrt(width * batch)
    rows = 2 * count
    dma = pltpu.SemaphoreType.DMA
    grads = pl.pallas_call(
        functools.partial(kernel, scale),
        out_shape=pltpu.VMEM((2, count, width), jnp.float32),
        in_specs=[pl.BlockSpec(memory_space=pltpu.HBM)] * 3,
        out_specs=pl.BlockSpec(memory_space=pltpu.VMEM),
        scratch_shapes=[
            pltpu.SMEM((2,), jnp.float32),
            pltpu.VMEM((2, count, width), jnp.bfloat16),
            pltpu.VMEM((PEERS + 1, rows, width), jnp.bfloat16),
            pltpu.VMEM((NZ, CORES, rows, width), jnp.bfloat16),
            pltpu.VMEM(((PEERS + 1) * rows, 2 * NZ * rows), jnp.bfloat16),
            pltpu.VMEM((PEERS, rows, width), jnp.bfloat16),
            pltpu.VMEM((PEERS, rows, width), jnp.bfloat16),
            pltpu.SemaphoreType.REGULAR((2,)),
            dma((3,)),
            dma, dma((len(ARRIVALS),)),
            dma, dma, dma, dma, dma, dma, dma, dma((PEERS // SHARE,)),
        ],
        compiler_params=pltpu.CompilerParams(collective_id=0, has_side_effects=True, vmem_limit_bytes=60 * 1024 * 1024),
    )(loss_weights, images, texts)
    return (grads[0], grads[1])


def solution(mesh):
    in_specs = (P(("row", "col"), None), P(("row", "col"), None), P())
    out_specs = (P(("row", "col"), None), P(("row", "col"), None))
    return jax.shard_map(local, mesh=mesh, in_specs=in_specs, out_specs=out_specs, check_vma=False)
```

```python
import functools
import math

import jax
import jax.numpy as jnp
from jax import lax
from jax.experimental import pallas as pl
from jax.experimental.pallas import tpu as pltpu
from jax.sharding import PartitionSpec as P

MESH = pl.DeviceIdType.MESH
NX, NY, NZ, CORES = 4, 4, 16, 2
HALF = NZ // 2


def ring_distance(step, size):
    return min(step, size - step)


PLANE = sorted(
    [(dx, dy) for dy in range(NY) for dx in range(NX)],
    key=lambda o: -(ring_distance(o[0], NX) + ring_distance(o[1], NY)),
)
PEERS = len(PLANE) - 1
SHARE = 5


def at_distance(distance):
    return [k for k, (dx, dy) in enumerate(PLANE) if ring_distance(dx, NX) + ring_distance(dy, NY) == distance]


NEAR = [(0, 3), (0, 1), (3, 3), (3, -1), (3, 1), (6, 2), (6, 1), (6, -1)]
HOPS = [hop for origin, step in NEAR for hop in ((origin, step), (-origin, -step))]
LINE_PEERS = sorted({step for _, step in HOPS})


def arrivals():
    level, order = {0: 0}, []
    for origin, step in NEAR:
        level[origin + step] = level[origin] + 1
    relays = [hop for hop in NEAR if any(origin == sum(hop) for origin, _ in NEAR)]
    for depth in sorted({level[sum(hop)] for hop in relays}):
        for c in (1, 0):
            for origin, step in relays:
                if level[origin + step] == depth:
                    order += [[(origin, step, c)], [(-origin, -step, c)]]
    leaves = [hop for hop in NEAR if hop not in relays]
    for depth in sorted({level[sum(hop)] for hop in leaves}):
        for c in (1, 0):
            for origin, step in leaves:
                if level[origin + step] == depth:
                    order.append([(origin, step, c), (-origin, -step, c)])
    return order


ARRIVALS = arrivals()


def urgent(hop):
    last = max(NEAR, key=lambda other: abs(sum(other)))[0]
    up = hop if hop in NEAR else (-hop[0], -hop[1])
    return any(origin == sum(up) for origin, _ in NEAR) or up[0] == last


def group_of(origin, step, c):
    return next(n for n, group in enumerate(ARRIVALS) if (origin, step, c) in group)


def kernel(scale, weights_hbm, img_hbm, txt_hbm, out, weights, own, xi, xj, w, part, inbox, news, load_sem, z_send, z_recv, hand_send, hand_recv, sib_send, sib_recv, i_send, i_recv, g_send, g_recv):
    rows, width = xi.shape[1:]
    half = width // 2
    row, col = lax.axis_index("row"), lax.axis_index("col")
    y, zh, core = row // 4, (row // 2) % 2, row % 2
    zl, x = col // NX, col % NX
    z = zh * 8 + zl

    def device(x, y, z, core):
        return (y * 4 + (z // 8) * 2 + core, (z % 8) * NX + x)

    sibling = device(x, y, z, 1 - core)
    line = {d: device(x, y, (z + d + NZ) % NZ, core) for d in LINE_PEERS}
    ahead = [[device((x + dx) % NX, (y + dy) % NY, z, c) for dx, dy in PLANE[:PEERS]] for c in range(CORES)]
    beside = [[device((x + dx) % NX, (y + dy) % NY, z, c) for dx, dy in [(1, 0), (NX - 1, 0), (0, 1), (0, NY - 1)]] for c in range(CORES)]
    behind = [device((x + NX - dx) % NX, (y + NY - dy) % NY, z, core) for dx, dy in PLANE[:PEERS]]

    loads = [
        pltpu.make_async_copy(img_hbm, own.at[0], load_sem.at[0]),
        pltpu.make_async_copy(txt_hbm, own.at[1], load_sem.at[1]),
        pltpu.make_async_copy(weights_hbm, weights, load_sem.at[2]),
    ]
    for load in loads:
        load.start()

    barrier = pltpu.get_barrier_semaphore()
    @pl.when(core == 1)
    def _():
        for peer in line.values():
            pl.semaphore_signal(barrier, inc=1, device_id=peer, device_id_type=MESH)

    for peer in [sibling] + beside[1]:
        pl.semaphore_signal(barrier, inc=1, device_id=peer, device_id_type=MESH)

    for load in loads:
        load.wait()
    block = own[...].astype(jnp.float32).reshape(rows, width).astype(jnp.bfloat16)
    xj[0, core] = block
    xi[PEERS] = block
    pl.semaphore_wait(barrier, core * (len(line) + 2 * len(beside[1])) + 1)

    def hop(origin, step, c):
        src, dst = origin % NZ, (origin + step) % NZ
        lanes = slice(None) if dst != HALF else pl.ds(0 if step > 0 else half, half)
        return pltpu.make_async_remote_copy(
            src_ref=xj.at[src, c, :, lanes], dst_ref=xj.at[dst, c, :, lanes], send_sem=z_send, recv_sem=z_recv.at[group_of(origin, step, c)],
            device_id=line[step], device_id_type=MESH)

    hand = pltpu.make_async_remote_copy(
        src_ref=xj.at[0, core], dst_ref=xj.at[0, core], send_sem=hand_send, recv_sem=hand_recv,
        device_id=sibling, device_id_type=MESH)

    def across(slot, c):
        return pltpu.make_async_remote_copy(
            src_ref=xj.at[slot, c], dst_ref=xj.at[slot, c], send_sem=sib_send, recv_sem=sib_recv,
            device_id=sibling, device_id_type=MESH)

    def spread(k, c):
        return pltpu.make_async_remote_copy(
            src_ref=xj.at[0, c], dst_ref=xi.at[k], send_sem=i_send, recv_sem=i_recv,
            device_id=ahead[c][k], device_id_type=MESH)

    def give(k):
        return pltpu.make_async_remote_copy(
            src_ref=part.at[k], dst_ref=inbox.at[k], send_sem=g_send, recv_sem=g_recv.at[k // SHARE],
            device_id=behind[k], device_id_type=MESH)

    def landed(ref, sem):
        pltpu.make_async_copy(ref, ref, sem).wait()

    def start(here, c, first):
        for onward in HOPS:
            if onward[0] == here and urgent(onward) == first:
                hop(*onward, c).start()

    second = at_distance(2)

    def spread_to(distance):
        for k in at_distance(distance):
            for c in range(CORES):
                spread(k, c).start()

    hand.start()

    @pl.when(core == 1)
    def _():
        for peer in beside[0]:
            pl.semaphore_signal(news.at[0], inc=1, device_id=peer, device_id_type=MESH)
        start(0, 1, True)

    hand.wait_recv()

    @pl.when(core == 0)
    def _():
        spread_to(1)
        pl.semaphore_wait(news.at[0], len(beside[0]))
        for k in second:
            pl.semaphore_signal(news.at[1], inc=1, device_id=ahead[0][k], device_id_type=MESH)
        spread_to(2)
        pl.semaphore_wait(news.at[1], len(second))
        spread_to(4)
        spread_to(3)

    @pl.when(core == 1)
    def _():
        start(0, 0, True)
        start(0, 1, False)
        start(0, 0, False)
        left = []
        for n, group in enumerate(ARRIVALS):
            landed(xj.at[0, pl.ds(0, 1)] if len(group) == 1 or sum(group[0][:2]) == HALF else xj.at[0], z_recv.at[n])
            for origin, step, c in group:
                here = origin + step
                start(here, c, True)
                left.append((here, c))
                if here != -HALF:
                    across(here % NZ, c).start()
            if len(group) == 1 and group[0][1] < 0 and group[0][2] == 0:
                for here, c in left:
                    start(here, c, False)
                left = []

    landed(xi.at[pl.ds(0, PEERS)], i_recv)
    pl.when(core == 0)(lambda: landed(xj.at[pl.ds(1, NZ - 1)], sib_recv))

    blocks = PEERS + 1
    keys = xj[...].reshape(2 * NZ * rows, width)
    scores = lax.dot_general(
        xi[...].reshape(blocks * rows, width), keys, (((1,), (1,)), ((), ())), preferred_element_type=jnp.float32)
    lanes = scores.shape[1]
    lane_kind = (lax.broadcasted_iota(jnp.int32, scores.shape, 1) // 8) % 2
    row_kind = (lax.broadcasted_iota(jnp.int32, scores.shape, 0) // 8) % 2
    turned = jnp.where(lane_kind == 0, pltpu.roll(scores, lanes - 8, 1), pltpu.roll(scores, 8, 1))
    turned = turned.reshape(blocks, 2, 8, lanes)
    turned = jnp.concatenate([turned[:, 1:], turned[:, :1]], axis=1).reshape(scores.shape)
    factor = jnp.where(lane_kind == row_kind, weights[1] * scale, weights[0] * scale)
    w[...] = ((scores - turned) * factor).astype(jnp.bfloat16)

    group = 4
    for first in range(0, blocks, group):
        total = jnp.dot(w[pl.ds(first * rows, group * rows), :], keys, preferred_element_type=jnp.float32)
        for k in range(first, first + group):
            block = total[(k - first) * rows : (k - first + 1) * rows]
            if k < PEERS:
                part[k] = block.astype(jnp.bfloat16)
                give(k).start()
            else:
                mine = block
    for first in range(0, PEERS, SHARE):
        landed(inbox.at[pl.ds(first, SHARE)], g_recv.at[first // SHARE])
        for k in range(first, first + SHARE):
            mine = mine + inbox[k].astype(jnp.float32)
    out[0] = mine[:8]
    out[1] = mine[8:]

    @pl.when(core == 1)
    def _():
        landed(xj.at[pl.ds(0, NZ - 1)], z_send)
        landed(xj.at[pl.ds(1, NZ - 1)], sib_send)

    hand.wait_send()

    @pl.when(core == 0)
    def _():
        landed(xj.at[pl.ds(0, PEERS)], i_send)

    landed(part, g_send)


def local(images, texts, loss_weights):
    count, width = images.shape
    batch = count * lax.axis_size("row") * lax.axis_size("col")
    scale = 1.0 / math.sqrt(width * batch)
    rows = 2 * count
    dma = pltpu.SemaphoreType.DMA
    grads = pl.pallas_call(
        functools.partial(kernel, scale),
        out_shape=pltpu.VMEM((2, count, width), jnp.float32),
        in_specs=[pl.BlockSpec(memory_space=pltpu.HBM)] * 3,
        out_specs=pl.BlockSpec(memory_space=pltpu.VMEM),
        scratch_shapes=[
            pltpu.SMEM((2,), jnp.float32),
            pltpu.VMEM((2, count, width), jnp.bfloat16),
            pltpu.VMEM((PEERS + 1, rows, width), jnp.bfloat16),
            pltpu.VMEM((NZ, CORES, rows, width), jnp.bfloat16),
            pltpu.VMEM(((PEERS + 1) * rows, 2 * NZ * rows), jnp.bfloat16),
            pltpu.VMEM((PEERS, rows, width), jnp.bfloat16),
            pltpu.VMEM((PEERS, rows, width), jnp.bfloat16),
            pltpu.SemaphoreType.REGULAR((2,)),
            dma((3,)),
            dma, dma((len(ARRIVALS),)),
            dma, dma, dma, dma, dma, dma, dma, dma((PEERS // SHARE,)),
        ],
        compiler_params=pltpu.CompilerParams(collective_id=0, has_side_effects=True, vmem_limit_bytes=60 * 1024 * 1024),
    )(loss_weights, images, texts)
    return (grads[0], grads[1])


def solution(mesh):
    in_specs = (P(("row", "col"), None), P(("row", "col"), None), P())
    out_specs = (P(("row", "col"), None), P(("row", "col"), None))
    return jax.shard_map(local, mesh=mesh, in_specs=in_specs, out_specs=out_specs, check_vma=False)
```
